768 devices in a mesh: gx: 24 (over z, core), gy: 4 (over x), gz: 8 (over y).
Axes of the slice: x: 4, y: 8, z: 12, core: 2. Of those that a mesh axis runs over, the one named last changes fastest.
Arguments:
- loads: bfloat16 [24, 4, 8, 1024, 256], P('gx', 'gy', 'gz'), may hold values from -6 to 6
- start: bfloat16 [24, 4, 8, 1024, 256], P('gx', 'gy', 'gz'), may hold values from -6 to 6
- interface_op: bfloat16 [24, 4, 8, 1024, 1024], P('gx', 'gy', 'gz'), as said below
- block_order: int32 [24, 4, 8, 8], P('gx', 'gy', 'gz'), may hold values from 0 to 7, each once within a row
- interface_weights: float32 [24, 4, 8, 1024], P('gx', 'gy', 'gz'), may hold values from 0.1 to 0.3
- coarse_modes: float32 [24, 4, 8, 32, 1024], P('gx', 'gy', 'gz'), as said below
- region_weights: float32 [24, 4, 8, 32, 16], P('gx', 'gy', 'gz'), as said below
- region_inverse: float32 [24, 1024, 1024], P('gx', ('gy', 'gz')), as said below
- root_inverse: float32 [384, 384], P('gx'), as said below
Outputs:
- solution: float32 [24, 4, 8, 1024, 256], P('gx', 'gy', 'gz')
The draws below stay inside these ranges and needn't reach their ends.
Inputs may be any that keep to these rules, and one draw needn't show every extreme that they name: `block_order`: each row lists every number from 0 to 7 once. `interface_op`: each subdomain's matrix has a dominant positive diagonal and full dense off-diagonal part. `region_inverse`: dense, with a dominant positive diagonal. `root_inverse`: dense, with a dominant positive diagonal. `coarse_modes`: dense. `region_weights`: dense.
All inputs are finite; a program needn't handle non-finite values.
Results may differ from the reference program's by a relative error of at most 0.0003.
Values sent between devices are 32-bit elements; how exact they have to be, the bound alone decides.
A program may use at most 32 MiB of HBM per device.

```python
import math
import jax
import jax.numpy as jnp
from jax import lax

BLOCK = 128
IFACE = 1024
CASES = 256
MODES = 32
RM = 16
ITERS = 2
SX = 24
SY = 4
SZ = 8
RORD = 1024
ROOT = 384


def dominant_matrix(key, count, order, diag_low, diag_high, spread):
    noise_key, diag_key = jax.random.split(key, 2)
    noise = jax.random.normal(noise_key, (count, order, order), jnp.float32)
    diagonal = jax.random.uniform(diag_key, (count, order), jnp.float32, diag_low, diag_high)
    return noise * (spread / order ** 0.5) + diagonal[:, :, None] * jnp.eye(order, dtype=jnp.float32)


def draw_interface_op(key, part):
    matrix = dominant_matrix(jax.random.fold_in(key, 11), SX * SY * SZ, IFACE, 1.5, 2.5, 0.6)
    return matrix.reshape(SX, SY, SZ, IFACE, IFACE).astype(jnp.bfloat16)


def draw_region_inverse(key, part):
    return dominant_matrix(jax.random.fold_in(key, 12), SX, RORD, 0.5, 1.5, 0.5)


def draw_root_inverse(key, part):
    return dominant_matrix(jax.random.fold_in(key, 13), 1, ROOT, 0.5, 1.5, 0.5)[0]


def draw_coarse_modes(key, part):
    inner = jax.random.fold_in(key, 14)
    scale = float(MODES * IFACE) ** (-0.25)
    values = jax.random.normal(inner, (SX, SY, SZ, MODES, IFACE), jnp.float32)
    return values * scale


def draw_region_weights(key, part):
    inner = jax.random.fold_in(key, 15)
    scale = float(RORD * RM) ** (-0.25)
    values = jax.random.normal(inner, (SX, SY, SZ, MODES, RM), jnp.float32)
    return values * scale


def levels(stream_key, shape, cuts, least, high):
    level, own = 1.0, jax.random.fold_in(stream_key, 6)
    for axis_at, parts in cuts:
        draws = jnp.exp(jax.random.uniform(jax.random.fold_in(own, axis_at), (parts,), jnp.float32, least / len(cuts), high / len(cuts)))
        level = level * jnp.repeat(draws, shape[axis_at] // parts).reshape([-1 if axis == axis_at else 1 for axis in range(len(shape))])
    return level


def centred(own_key, dims, width, most, cuts=(), kind=jnp.bfloat16):
    level = levels(own_key, dims, cuts, -0.22, 0.18) if cuts else 1.0
    drawn = jax.random.normal(own_key, dims, jnp.float32) * width * level
    return jnp.minimum(jnp.maximum(drawn, -most), most).astype(kind)


def setup_inputs(seed: int = 0) -> dict:
    splits = jax.random.split(jax.random.key(seed), 10)
    loads = centred(splits[0], (SX, SY, SZ, IFACE, CASES), 1.0, 6.0, ((0, 24), (1, 4), (2, 8)))
    start = centred(splits[1], (SX, SY, SZ, IFACE, CASES), 1.0, 6.0, ((0, 24), (1, 4), (2, 8)))
    interface_op = draw_interface_op(jax.random.fold_in(splits[9], 71), 0)
    block_order = jax.vmap(lambda own: jax.random.permutation(own, 8))(jax.random.split(splits[3], SX * SY * SZ)).reshape((SX, SY, SZ, 8)).astype(jnp.int32)
    interface_weights = jnp.clip(jnp.exp(math.log(0.3) - 1.0986123 * jax.random.uniform(splits[4], (SX, SY, SZ, IFACE), jnp.float32) ** levels(splits[4], (SX, SY, SZ, IFACE), ((0, 24), (1, 4), (2, 8)), -0.2, 0.2)), 0.1, 0.3)
    coarse_modes = draw_coarse_modes(jax.random.fold_in(splits[9], 71), 0)
    region_weights = draw_region_weights(jax.random.fold_in(splits[9], 71), 0)
    region_inverse = draw_region_inverse(jax.random.fold_in(splits[9], 71), 0)
    root_inverse = draw_root_inverse(jax.random.fold_in(splits[9], 71), 0)
    return dict(loads=loads, start=start, interface_op=interface_op, block_order=block_order, interface_weights=interface_weights, coarse_modes=coarse_modes, region_weights=region_weights, region_inverse=region_inverse, root_inverse=root_inverse)


HIGH = lax.Precision.HIGHEST


def apply_local(operator, local_iter, order):
    def single(items):
        matrix, values, perm = items
        blocks = values.reshape(8, BLOCK, CASES)
        gathered = blocks[perm].reshape(8 * BLOCK, CASES)
        result = jnp.dot(matrix, gathered, preferred_element_type=jnp.float32).reshape(8, BLOCK, CASES)
        return jnp.zeros_like(result).at[perm].set(result)

    count = SX * SY * SZ
    outputs = lax.map(single, (operator.reshape(count, IFACE, IFACE), local_iter.reshape(count, IFACE, CASES), order.reshape(count, 8)))
    return outputs.reshape(SX, SY, SZ, 8, BLOCK, CASES)


def assemble(product):
    result = product
    result = result.at[1:, :, :, 0].add(product[:-1, :, :, 1])
    result = result.at[:-1, :, :, 1].add(product[1:, :, :, 0])
    result = result.at[:, 1:, :, 2].add(product[:, :-1, :, 3])
    result = result.at[:, :-1, :, 3].add(product[:, 1:, :, 2])
    result = result.at[:, :, 1:, 4].add(product[:, :, :-1, 5])
    result = result.at[:, :, :-1, 5].add(product[:, :, 1:, 4])
    return result.reshape(SX, SY, SZ, IFACE, CASES)


def reference(loads, start, interface_op, block_order, interface_weights, coarse_modes, region_weights, region_inverse, root_inverse):
    solution = start.astype(jnp.float32)
    for step in range(ITERS):
        local_iter = solution.astype(jnp.bfloat16)
        product = apply_local(interface_op, local_iter, block_order)
        assembled = assemble(product)
        residual = loads.astype(jnp.float32) - assembled
        coarse = jnp.einsum("abcmi,abcin->abcmn", coarse_modes, residual, precision=HIGH)
        stacked = coarse.reshape(SX, RORD, CASES)
        region_part = jnp.einsum("xij,xjn->xin", region_inverse, stacked, precision=HIGH).reshape(SX, SY, SZ, MODES, CASES)
        root_input = jnp.einsum("abcmk,abcmn->akn", region_weights, coarse, precision=HIGH).reshape(ROOT, CASES)
        root_part = jnp.dot(root_inverse, root_input, precision=HIGH).reshape(SX, RM, CASES)
        amplitude = region_part + jnp.einsum("abcmk,akn->abcmn", region_weights, root_part, precision=HIGH)
        solution = solution + interface_weights[..., None] * residual + jnp.einsum("abcmi,abcmn->abcin", coarse_modes, amplitude, precision=HIGH)
    return solution
```

```python
import functools

import jax
import jax.numpy as jnp
from jax import lax
from jax.experimental import pallas as pl
from jax.experimental.pallas import tpu as pltpu
from jax.sharding import PartitionSpec as P

ITERS = 2
MESH = pl.DeviceIdType.MESH
F32 = jnp.float32
BF16 = jnp.bfloat16
HIGH = lax.Precision.HIGHEST
PAIRS = ((2, 3), (4, 5), (0, 1), (6, 7))


def dot(a, b):
    return jnp.dot(a, b, preferred_element_type=F32)


def split3(x):
    high = x.astype(BF16)
    rest = x - high.astype(F32)
    mid = rest.astype(BF16)
    low = (rest - mid.astype(F32)).astype(BF16)
    return high, mid, low


def split_rows(x):
    return jnp.concatenate([t.astype(F32) for t in split3(x)], axis=0).astype(BF16)


def rows_dot(left, right):
    n = left.shape[0] // 3
    high, mid, low = split3(right)
    p = dot(left, high)
    q = dot(left[: 2 * n], mid)
    r = dot(left[:n], low)
    return ((r + q[n:]) + p[2 * n :]) + (q[:n] + p[n : 2 * n]) + p[:n]


def deep_left(x, depth):
    high, mid, low = (t.astype(F32) for t in split3(x))
    terms = [high, high, mid, high, mid, low]
    fill = depth - 6 * x.shape[0]
    if fill:
        terms.append(jnp.zeros((fill, x.shape[1]), F32))
    return jnp.concatenate(terms, axis=0).T.astype(BF16)


def deep_right(x, depth):
    high, mid, low = split3(x)
    terms = [high, mid, high, low, mid, high]
    fill = depth - 6 * x.shape[0]
    if fill:
        terms.append(jnp.zeros((fill, x.shape[1]), BF16))
    return jnp.concatenate(terms, axis=0)


def pad_to(n, m):
    return -(-n // m) * m


def kernel(
    nx, ny, nz,
    perm_s, loads_h, start_h, op_h, w_h, modes_h, rw_h, rinv_h, root_h,
    base_o, g_o, root_o,
    loads_v, start_v, op_v, w_v, modes_v, rw_v,
    local, prod, halo, sol, solb, res, wb, modes_s, modes_t, g_t,
    rblk, rblk_s, rinv2, rinv_s,
    t_all, c_all, s_all, rp_send, rp_all, z_all, p_send, p_recv, root_v,
    in_sem, hs, hr, ts, tr, cs, cr, ss, sr, zs, zr, rs, rr, ps, pr, ms, mr, xs, xr, out_sem,
):
    gx, gy, gz = lax.axis_index("gx"), lax.axis_index("gy"), lax.axis_index("gz")
    nchip = nx // 2
    chip, core = gx // 2, lax.rem(gx, 2)
    modes_n, iface = modes_v.shape
    block = iface // 8
    width = nz * modes_n
    mate = (gx + 1 - 2 * core, gy, gz)
    beside = (lax.rem(gx + 2 * core - 1 + nx, nx), gy, gz)

    def along_z(off):
        return (gx, gy, lax.rem(gz + off, nz))

    def along_y(off):
        return (gx, lax.rem(gy + off, ny), gz)

    def along_x(off):
        return (lax.rem(chip + off, nchip) * 2 + core, gy, gz)

    def far_first(n):
        return sorted(range(1, n), key=lambda o: -min(o, n - o))

    def remote(src, dst, send, recv, device):
        return pltpu.make_async_remote_copy(
            src_ref=src, dst_ref=dst, send_sem=send, recv_sem=recv,
            device_id=device, device_id_type=MESH,
        )

    def columns(a):
        return pl.ds(pl.multiple_of(a * width, 128), width)

    loaded = {}
    for i, (name, src, dst) in enumerate((
        ("start", start_h, start_v), ("op", op_h, op_v), ("modes", modes_h, modes_v), ("rw", rw_h, rw_v),
        ("loads", loads_h, loads_v), ("w", w_h, w_v), ("root", root_h, rinv2.at[0]),
        ("rinv", rinv_h.at[:, columns(gy)], rblk.at[gy]),
    )):
        loaded[name] = pltpu.make_async_copy(src, dst, in_sem.at[i])
        loaded[name].start()

    barrier = pltpu.get_barrier_semaphore()
    greeted = (
        [along_x(o) for o in far_first(nchip)] + [along_z(o) for o in far_first(nz)]
        + [along_y(o) for o in far_first(ny)] + [beside, mate]
    )
    for device in greeted:
        pl.semaphore_signal(barrier, inc=1, device_id=device, device_id_type=MESH)

    has = (gx > 0, gx < nx - 1, gy > 0, gy < ny - 1, gz > 0, gz < nz - 1)
    towards = (
        (lax.rem(gx + nx - 1, nx), gy, gz), (lax.rem(gx + 1, nx), gy, gz),
        along_y(ny - 1), along_y(1), along_z(nz - 1), along_z(1),
    )

    def halo_copy(it, f):
        return remote(
            prod.at[it, f], halo.at[it, f ^ 1], hs.at[it, f], hr.at[it, f ^ 1], towards[f]
        )

    for it in range(ITERS):
        for f in range(6):

            @pl.when(jnp.logical_not(has[f]))
            def _(it=it, f=f):
                halo[it, f] = jnp.zeros_like(halo[it, f])

    perm = [perm_s[j] for j in range(8)]
    inverse = []
    for f in range(8):
        at = jnp.int32(0)
        for j in range(8):
            at = jnp.where(perm[j] == f, j, at)
        inverse.append(at)

    def send_pair(it, pair):
        for f in pair:
            if f < 6:

                @pl.when(has[f])
                def _(it=it, f=f):
                    halo_copy(it, f).start()

    def t_copy(it, off):
        return remote(
            t_all.at[it, gz], t_all.at[it, gz], ts.at[it, off], tr.at[it, off], along_z(off)
        )

    def c_copy(it, off):
        return remote(
            c_all.at[it, gz], c_all.at[it, gz], cs.at[it, off], cr.at[it, off], along_z(off)
        )

    def s_copy(it, off):
        return remote(
            s_all.at[it, gy], s_all.at[it, gy], ss.at[it, off], sr.at[it, off], along_y(off)
        )

    def z_copy(it, off):
        return remote(
            z_all.at[it, gx], z_all.at[it, gx], zs.at[it, off], zr.at[it, off], along_x(off)
        )

    def r_copy(off):
        to = along_y(off)
        return remote(rinv_h.at[:, columns(to[1])], rblk.at[gy], rs.at[off], rr.at[off], to)

    def rp_copy(it, off):
        to = along_y(off)
        return remote(
            rp_send.at[it, to[1]], rp_all.at[it, gy], ps.at[it, off], pr.at[it, off], to
        )

    def m_copy(it):
        return remote(p_send.at[it], p_recv.at[it], ms.at[it], mr.at[it], mate)

    root_copy = remote(root_h, rinv2.at[1], xs, xr, mate)

    for it in range(ITERS):
        if it == 0:
            loaded["start"].wait()
        for j in range(8):
            source = start_v if it == 0 else solb
            local[j * block : (j + 1) * block, :] = source[perm[j]]
        if it == 0:
            loaded["op"].wait()
        right = local[...]
        for pair in PAIRS:
            left = jnp.concatenate([op_v[inverse[f]] for f in pair], axis=0)
            both = dot(left, right)
            for k, f in enumerate(pair):
                prod[it, f] = both[k * block : (k + 1) * block]
            if it:
                send_pair(it, pair)
        if it == 0:
            loaded["modes"].wait()
            loaded["loads"].wait()
            loaded["rw"].wait()
            modes_s[...] = split_rows(modes_v[...])
            pl.semaphore_wait(barrier, len(greeted))
            for pair in PAIRS:
                send_pair(it, pair)
            root_copy.start()
            for off in range(1, ny):
                r_copy(off).start()
            modes_t[...] = deep_left(modes_v[...], modes_t.shape[1])
            g = jnp.dot(rw_v[...], modes_v[...], precision=HIGH, preferred_element_type=F32)
            g_t[...] = deep_left(g, g_t.shape[1])
            loaded["w"].wait()
            for f in range(8):
                wb[f] = jnp.broadcast_to(w_v[f : f + 1, :], (block, block)).T
            for k in range(nchip):
                for i in range(ITERS):
                    z_all[i, 2 * k + 1 - core] = jnp.zeros(z_all.shape[2:], F32)
            g_out = pltpu.make_async_copy(g_t, g_o, out_sem.at[0])
            g_out.start()

        coarse = None
        for pair in (PAIRS[3], PAIRS[2], PAIRS[0], PAIRS[1]):
            for f in pair:
                if f < 6:

                    @pl.when(has[f])
                    def _(it=it, f=f):
                        halo_copy(it, f ^ 1).wait_recv()

                    res[f] = loads_v[f].astype(F32) - (prod[it, f] + halo[it, f])
                else:
                    res[f] = loads_v[f].astype(F32) - prod[it, f]
            f = pair[0]
            part = rows_dot(
                modes_s[:, f * block : (f + 2) * block], res[f : f + 2].reshape(2 * block, -1)
            )
            coarse = part if coarse is None else coarse + part
        c_all[it, gz] = coarse
        t_all[it, gz] = jnp.dot(
            rw_v[...], coarse, precision=HIGH, preferred_element_type=F32
        )
        for off in far_first(nz):
            t_copy(it, off).start()
        for off in far_first(nz):
            c_copy(it, off).start()
        if it == 0:
            for off in range(1, ny):
                r_copy(off).wait_recv()
            loaded["rinv"].wait()
            rblk_s[...] = split_rows(rblk[...].reshape(rblk_s.shape[0] // 3, -1))
            root_copy.wait_recv()
            loaded["root"].wait()
            rinv_s[...] = split_rows(rinv2[...].reshape(rinv_s.shape[0] // 3, -1))
        for off in range(1, nz):
            t_copy(it, off).wait_recv()
        total = t_all[it, 0]
        for b in range(1, nz):
            total = total + t_all[it, b]
        s_all[it, gy] = total
        for off in far_first(ny):
            s_copy(it, off).start()
        for off in range(1, ny):
            s_copy(it, off).wait_recv()
        total = s_all[it, 0]
        for a in range(1, ny):
            total = total + s_all[it, a]
        z_all[it, gx] = total
        for off in far_first(nchip):
            z_copy(it, off).start()
        for off in range(1, nz):
            c_copy(it, off).wait_recv()
        part = rows_dot(rblk_s[...], c_all[it].reshape(width, -1))
        rp_send[it] = part.reshape(rp_send.shape[1:])
        rp_all[it, gy] = rp_send[it, gy]
        for off in far_first(ny):
            rp_copy(it, off).start()
        for f in range(8):
            old = start_v[f].astype(F32) if it == 0 else sol[f]
            scale = wb[f]
            sol[f] = old + jnp.concatenate([scale] * (old.shape[1] // block), axis=1) * res[f]
        for off in range(1, ny):
            rp_copy(it, off).wait_recv()
        region = rp_all[it, 0]
        for a in range(1, ny):
            region = region + rp_all[it, a]
        depth = modes_t.shape[1]
        sol[...] = sol[...] + dot(modes_t[...], deep_right(region, depth)).reshape(sol.shape)
        if it == ITERS - 1:
            base_out = pltpu.make_async_copy(sol, base_o, out_sem.at[1])
            base_out.start()
        for off in range(1, nchip):
            z_copy(it, off).wait_recv()
        stack = z_all[it].reshape(nx * z_all.shape[2], -1)
        both = rows_dot(rinv_s[...], stack)
        rm = both.shape[0] // 2
        p_send[it] = both[rm:]
        m_copy(it).start()
        m_copy(it).wait_recv()
        root = both[:rm] + p_recv[it]
        if it < ITERS - 1:
            depth = g_t.shape[1]
            new = sol[...] + dot(g_t[...], deep_right(root, depth)).reshape(sol.shape)
            sol[...] = new
            solb[...] = new.astype(BF16)
        else:
            root_v[...] = root

    root_out = pltpu.make_async_copy(root_v, root_o, out_sem.at[2])
    root_out.start()
    for it in range(ITERS):
        for f in range(6):

            @pl.when(has[f])
            def _(it=it, f=f):
                halo_copy(it, f).wait_send()

        for off in range(1, nz):
            t_copy(it, off).wait_send()
            c_copy(it, off).wait_send()
        for off in range(1, ny):
            s_copy(it, off).wait_send()
            rp_copy(it, off).wait_send()
        for off in range(1, nchip):
            z_copy(it, off).wait_send()
        m_copy(it).wait_send()
    for off in range(1, ny):
        r_copy(off).wait_send()
    root_copy.wait_send()
    g_out.wait()
    base_out.wait()
    root_out.wait()


def last_update(base, g, root, out):
    out[...] = base[...] + dot(g[...], deep_right(root[...], g.shape[1]))


def per_device(
    nx, ny, nz, loads, start, interface_op, block_order, interface_weights, coarse_modes,
    region_weights, region_inverse, root_inverse,
):
    iface, cases = loads.shape[-2:]
    block = iface // 8
    modes_n, rm = region_weights.shape[-2:]
    nchip = nx // 2
    width = nz * modes_n
    faces = (8, block, cases)
    deep_m, deep_g = pad_to(6 * modes_n, 128), pad_to(6 * rm, 128)
    any_spec = pl.BlockSpec(memory_space=pltpu.HBM)
    dma = pltpu.SemaphoreType.DMA
    base, g, root = pl.pallas_call(
        functools.partial(kernel, nx, ny, nz),
        out_shape=(
            jax.ShapeDtypeStruct(faces, F32),
            jax.ShapeDtypeStruct((iface, deep_g), BF16),
            jax.ShapeDtypeStruct((rm, cases), F32),
        ),
        in_specs=[pl.BlockSpec(memory_space=pltpu.SMEM)] + [any_spec] * 8,
        out_specs=(any_spec,) * 3,
        scratch_shapes=[
            pltpu.VMEM(faces, BF16),
            pltpu.VMEM(faces, BF16),
            pltpu.VMEM((8, block, iface), BF16),
            pltpu.VMEM((8, block), F32),
            pltpu.VMEM((modes_n, iface), F32),
            pltpu.VMEM((rm, modes_n), F32),
            pltpu.VMEM((iface, cases), BF16),
            pltpu.VMEM((ITERS, *faces), F32),
            pltpu.VMEM((ITERS, 6, block, cases), F32),
            pltpu.VMEM(faces, F32),
            pltpu.VMEM(faces, BF16),
            pltpu.VMEM(faces, F32),
            pltpu.VMEM((8, block, block), F32),
            pltpu.VMEM((3 * modes_n, iface), BF16),
            pltpu.VMEM((iface, deep_m), BF16),
            pltpu.VMEM((iface, deep_g), BF16),
            pltpu.VMEM((ny, modes_n, width), F32),
            pltpu.VMEM((3 * ny * modes_n, width), BF16),
            pltpu.VMEM((2, rm, nx * rm), F32),
            pltpu.VMEM((6 * rm, nx * rm), BF16),
            pltpu.VMEM((ITERS, nz, rm, cases), F32),
            pltpu.VMEM((ITERS, nz, modes_n, cases), F32),
            pltpu.VMEM((ITERS, ny, rm, cases), F32),
            pltpu.VMEM((ITERS, ny, modes_n, cases), F32),
            pltpu.VMEM((ITERS, ny, modes_n, cases), F32),
            pltpu.VMEM((ITERS, nx, rm, cases), F32),
            pltpu.VMEM((ITERS, rm, cases), F32),
            pltpu.VMEM((ITERS, rm, cases), F32),
            pltpu.VMEM((rm, cases), F32),
            dma((8,)),
            dma((ITERS, 6)), dma((ITERS, 6)),
            dma((ITERS, nz)), dma((ITERS, nz)),
            dma((ITERS, nz)), dma((ITERS, nz)),
            dma((ITERS, ny)), dma((ITERS, ny)),
            dma((ITERS, nchip)), dma((ITERS, nchip)),
            dma((ny,)), dma((ny,)),
            dma((ITERS, ny)), dma((ITERS, ny)),
            dma((ITERS,)), dma((ITERS,)),
            dma(()), dma(()),
            dma((3,)),
        ],
        compiler_params=pltpu.CompilerParams(
            collective_id=0, has_side_effects=True, vmem_limit_bytes=67043328
        ),
        name="iterate",
    )(
        block_order.reshape(8),
        loads.reshape(faces),
        start.reshape(faces),
        interface_op.reshape(8, block, iface),
        interface_weights.reshape(8, block),
        coarse_modes.reshape(modes_n, iface),
        region_weights.reshape(modes_n, rm).T,
        region_inverse.reshape(modes_n, -1),
        root_inverse,
    )
    steps = 4
    out = pl.pallas_call(
        last_update,
        grid=(steps,),
        out_shape=jax.ShapeDtypeStruct((iface, cases), F32),
        in_specs=[
            pl.BlockSpec((iface // steps, cases), lambda i: (i, 0)),
            pl.BlockSpec((iface // steps, deep_g), lambda i: (i, 0)),
            pl.BlockSpec((rm, cases), lambda i: (0, 0)),
        ],
        out_specs=pl.BlockSpec((iface // steps, cases), lambda i: (i, 0)),
        name="last_update",
    )(base.reshape(iface, cases), g, root)
    return out.reshape(1, 1, 1, iface, cases)


def solution(mesh):
    nx, ny, nz = (mesh.shape[axis] for axis in ("gx", "gy", "gz"))
    placed = (
        P("gx", "gy", "gz", None, None),
        P("gx", "gy", "gz", None, None),
        P("gx", "gy", "gz", None, None),
        P("gx", "gy", "gz", None),
        P("gx", "gy", "gz", None),
        P("gx", "gy", "gz", None, None),
        P("gx", "gy", "gz", None, None),
        P("gx", ("gy", "gz"), None),
        P("gx", None),
    )
    return jax.shard_map(
        functools.partial(per_device, nx, ny, nz),
        mesh=mesh,
        in_specs=placed,
        out_specs=P("gx", "gy", "gz", None, None),
        check_vma=False,
    )
```

```python
import functools

import jax
import jax.numpy as jnp
from jax import lax
from jax.experimental import pallas as pl
from jax.experimental.pallas import tpu as pltpu
from jax.sharding import PartitionSpec as P

ITERS = 2
MESH = pl.DeviceIdType.MESH
F32 = jnp.float32
BF16 = jnp.bfloat16
HIGH = lax.Precision.HIGHEST
PAIRS = ((2, 3), (4, 5), (0, 1), (6, 7))


def dot(a, b):
    return jnp.dot(a, b, preferred_element_type=F32)


def split3(x):
    high = x.astype(BF16)
    rest = x - high.astype(F32)
    mid = rest.astype(BF16)
    low = (rest - mid.astype(F32)).astype(BF16)
    return high, mid, low


def split_rows(x):
    return jnp.concatenate([t.astype(F32) for t in split3(x)], axis=0).astype(BF16)


def rows_dot(left, right):
    n = left.shape[0] // 3
    high, mid, low = split3(right)
    p = dot(left, high)
    q = dot(left[: 2 * n], mid)
    r = dot(left[:n], low)
    return ((r + q[n:]) + p[2 * n :]) + (q[:n] + p[n : 2 * n]) + p[:n]


def deep_left(x, depth):
    high, mid, low = (t.astype(F32) for t in split3(x))
    terms = [high, high, mid, high, mid, low]
    fill = depth - 6 * x.shape[0]
    if fill:
        terms.append(jnp.zeros((fill, x.shape[1]), F32))
    return jnp.concatenate(terms, axis=0).T.astype(BF16)


def deep_right(x, depth):
    high, mid, low = split3(x)
    terms = [high, mid, high, low, mid, high]
    fill = depth - 6 * x.shape[0]
    if fill:
        terms.append(jnp.zeros((fill, x.shape[1]), BF16))
    return jnp.concatenate(terms, axis=0)


def pad_to(n, m):
    return -(-n // m) * m


def kernel(
    nx, ny, nz,
    perm_s, loads_h, start_h, op_h, w_h, modes_h, rw_h, rinv_h, root_h,
    base_o, g_o, root_o,
    loads_v, start_v, op_v, w_v, modes_v, rw_v,
    local, prod, halo, sol, solb, wb, pair_s, modes_t, g_t, nbm,
    rblk, rblk_s, rinv2, rinv_s,
    kb_send, kb, t_send, tx, ty, c_all, rp_send, rp_all, z_all, f_send, f_all, root_v,
    in_sem, hs, hr, ns, nr, ks, kr, ts, tr, ys, yr, cs, cr, zs, zr, rs, rr, ps, pr, fs, fr, xs, xr,
    out_sem,
):
    gx, gy, gz = lax.axis_index("gx"), lax.axis_index("gy"), lax.axis_index("gz")
    nchip = nx // 2
    chip, core = gx // 2, lax.rem(gx, 2)
    half = gy // 2
    modes_n, iface = modes_v.shape
    block = iface // 8
    width = nz * modes_n
    mate_x = gx + 1 - 2 * core
    mate = (mate_x, gy, gz)
    beside = (lax.rem(gx + 2 * core - 1 + nx, nx), gy, gz)

    def along_z(off):
        return (gx, gy, lax.rem(gz + off, nz))

    def along_y(off, x=gx):
        return (x, lax.rem(gy + off, ny), gz)

    def along_x(off):
        return (lax.rem(chip + off, nchip) * 2 + core, gy, gz)

    def far_first(n):
        return sorted(range(1, n), key=lambda o: -min(o, n - o))

    def remote(src, dst, send, recv, device):
        return pltpu.make_async_remote_copy(
            src_ref=src, dst_ref=dst, send_sem=send, recv_sem=recv,
            device_id=device, device_id_type=MESH,
        )

    def columns(a):
        return pl.ds(pl.multiple_of(a * width, 128), width)

    loaded = {}
    for i, (name, src, dst) in enumerate((
        ("start", start_h, start_v), ("op", op_h, op_v), ("modes", modes_h, modes_v), ("rw", rw_h, rw_v),
        ("loads", loads_h, loads_v), ("w", w_h, w_v), ("root", root_h, rinv2.at[0]),
        ("rinv", rinv_h.at[:, columns(gy)], rblk.at[gy]),
    )):
        loaded[name] = pltpu.make_async_copy(src, dst, in_sem.at[i])
        loaded[name].start()

    barrier = pltpu.get_barrier_semaphore()
    greeted = (
        [along_x(o) for o in far_first(nchip)] + [along_z(o) for o in far_first(nz)]
        + [along_y(o) for o in far_first(ny)] + [along_y(o, mate_x) for o in far_first(ny)]
        + [beside, mate]
    )
    for device in greeted:
        pl.semaphore_signal(barrier, inc=1, device_id=device, device_id_type=MESH)

    has = (gx > 0, gx < nx - 1, gy > 0, gy < ny - 1, gz > 0, gz < nz - 1)
    towards = (
        (lax.rem(gx + nx - 1, nx), gy, gz), (lax.rem(gx + 1, nx), gy, gz),
        along_y(ny - 1), along_y(1), along_z(nz - 1), along_z(1),
    )

    def halo_copy(it, f):
        return remote(
            prod.at[it, f], halo.at[it, f ^ 1], hs.at[it, f], hr.at[it, f ^ 1], towards[f]
        )

    def modes_copy(f):
        face = modes_h.at[:, f * block : (f + 1) * block]
        return remote(face, nbm.at[f ^ 1], ns.at[f], nr.at[f ^ 1], towards[f])

    def kb_copy(it, f):
        return remote(
            kb_send.at[it, f], kb.at[it, f ^ 1], ks.at[it, f], kr.at[it, f ^ 1], towards[f]
        )

    def t_copy(it, off):
        to = along_y(off)
        return remote(t_send.at[it, to[1]], tx.at[it, gy], ts.at[it, off], tr.at[it, off], to)

    def y_copy(it, off):
        return remote(ty.at[it, gz], ty.at[it, gz], ys.at[it, off], yr.at[it, off], along_z(off))

    def c_copy(it, off):
        return remote(
            c_all.at[it, gz], c_all.at[it, gz], cs.at[it, off], cr.at[it, off], along_z(off)
        )

    def z_rows(h):
        return pl.ds(pl.multiple_of(h * 8, 8), 8)

    def z_copy(it, off):
        tile = z_all.at[it, gx, z_rows(half)]
        return remote(tile, tile, zs.at[it, off], zr.at[it, off], along_x(off))

    def r_copy(off):
        to = along_y(off)
        return remote(rinv_h.at[:, columns(to[1])], rblk.at[gy], rs.at[off], rr.at[off], to)

    def rp_copy(it, off):
        to = along_y(off)
        return remote(
            rp_send.at[it, to[1]], rp_all.at[it, gy], ps.at[it, off], pr.at[it, off], to
        )

    def f_copy(it, other, off):
        at = (it, other, off)
        to = along_y(off, mate_x if other else gx)
        return remote(f_send.at[it, other], f_all.at[it, core, gy], fs.at[at], fr.at[at], to)

    root_copy = remote(root_h, rinv2.at[1], xs, xr, mate)
    finals = [(1, o) for o in (2, 1, 3, 0) if o < ny] + [(0, o) for o in far_first(ny)]

    for f in range(6):

        @pl.when(jnp.logical_not(has[f]))
        def _(f=f):
            nbm[f] = jnp.zeros_like(nbm[f])
            for it in range(ITERS):
                halo[it, f] = jnp.zeros_like(halo[it, f])
                kb[it, f] = jnp.zeros_like(kb[it, f])

    perm = [perm_s[j] for j in range(8)]
    inverse = []
    for f in range(8):
        at = jnp.int32(0)
        for j in range(8):
            at = jnp.where(perm[j] == f, j, at)
        inverse.append(at)

    def on_faces(faces, action):
        for f in faces:
            if f < 6:

                @pl.when(has[f])
                def _(f=f):
                    action(f)

    loads_c = None
    for it in range(ITERS):

        def products(it, pair):
            left = jnp.concatenate([op_v[inverse[f]] for f in pair], axis=0)
            both = dot(left, local[...])
            for k, f in enumerate(pair):
                prod[it, f] = both[k * block : (k + 1) * block]

        def contributions(it, p):
            pair = PAIRS[p]
            rows = 3 * modes_n * (3 if pair[0] < 6 else 1)
            got = rows_dot(
                pair_s[p, :rows], prod[it, pair[0] : pair[0] + 2].reshape(2 * block, -1)
            )
            if pair[0] < 6:
                kb_send[it, pair[0]] = got[modes_n : 2 * modes_n]
                kb_send[it, pair[1]] = got[2 * modes_n :]
                on_faces(pair, lambda f: kb_copy(it, f).start())
            return got[:modes_n]

        if it == 0:
            loaded["start"].wait()
        for j in range(8):
            source = start_v if it == 0 else solb
            local[j * block : (j + 1) * block, :] = source[perm[j]]
        own = []
        if it == 0:
            loaded["op"].wait()
            for pair in PAIRS:
                products(it, pair)
            loaded["modes"].wait()
            loaded["loads"].wait()
            loaded["rw"].wait()
            pl.semaphore_wait(barrier, len(greeted))
            on_faces(range(6), lambda f: modes_copy(f).start())
            modes_rows = split_rows(modes_v[...])
            loads_c = None
            for f in range(8):
                got = dot(modes_rows[:, f * block : (f + 1) * block], loads_v[f])
                loads_c = got if loads_c is None else loads_c + got
            n = modes_n
            loads_c = (loads_c[2 * n :] + loads_c[n : 2 * n]) + loads_c[:n]
            modes_t[...] = deep_left(modes_v[...], modes_t.shape[1])
            g = jnp.dot(rw_v[...], modes_v[...], precision=HIGH, preferred_element_type=F32)
            g_t[...] = deep_left(g, g_t.shape[1])
            loaded["w"].wait()
            for f in range(8):
                wb[f] = jnp.broadcast_to(w_v[f : f + 1, :], (block, block)).T
            pair_s[3, : 3 * n] = modes_rows[:, 6 * block :]
            for p in range(3):
                pair = PAIRS[p]
                on_faces(pair, lambda f: modes_copy(f ^ 1).wait_recv())
                fill = jnp.zeros((n, block), F32)
                pair_s[p] = split_rows(
                    jnp.concatenate([
                        modes_v[:, pair[0] * block : (pair[0] + 2) * block],
                        jnp.concatenate([nbm[pair[0]], fill], axis=1),
                        jnp.concatenate([fill, nbm[pair[1]]], axis=1),
                    ], axis=0)
                )
                own.append(contributions(it, p))
            own.append(contributions(it, 3))
        else:
            for p, pair in enumerate(PAIRS):
                products(it, pair)
                own.append(contributions(it, p))
        on_faces((2, 3, 0, 1), lambda f: halo_copy(it, f).start())
        if it == 0:
            root_copy.start()
            for off in range(1, ny):
                r_copy(off).start()
            for i in range(ITERS):
                for k in range(nchip):
                    z_all[i, 2 * k + 1 - core] = jnp.zeros(z_all.shape[2:], F32)
                    z_all[i, 2 * k + core, z_rows(1 - half)] = jnp.zeros((8, z_all.shape[3]), F32)
            g_out = pltpu.make_async_copy(g_t, g_o, out_sem.at[0])
            g_out.start()

        coarse = loads_c - (own[0] + own[1] + own[2] + own[3])
        for f in (0, 1, 2, 3, 4, 5):
            on_faces((f,), lambda f: kb_copy(it, f ^ 1).wait_recv())
            coarse = coarse - kb[it, f]
        c_all[it, gz] = coarse
        t = jnp.dot(rw_v[...], coarse, precision=HIGH, preferred_element_type=F32)
        lanes = t.shape[1] // 2
        for q in range(4):
            t_send[it, q] = t[8 * (q // 2) : 8 * (q // 2) + 8, lanes * (q % 2) : lanes * (q % 2 + 1)]
        for off in far_first(ny):
            t_copy(it, off).start()
        tx[it, gy] = t_send[it, gy]
        for off in range(1, ny):
            t_copy(it, off).wait_recv()
        total = tx[it, 0]
        for a in range(1, ny):
            total = total + tx[it, a]
        ty[it, gz] = total
        for off in far_first(nz):
            y_copy(it, off).start()
        for off in far_first(nz):
            c_copy(it, off).start()
        on_faces((4, 5), lambda f: halo_copy(it, f).start())
        if it == 0:
            for off in range(1, ny):
                r_copy(off).wait_recv()
            loaded["rinv"].wait()
            rblk_s[...] = split_rows(rblk[...].reshape(rblk_s.shape[0] // 3, -1))
            root_copy.wait_recv()
            loaded["root"].wait()
            rinv_s[...] = split_rows(rinv2[...].reshape(rinv_s.shape[0] // 3, -1))
        for off in range(1, nz):
            y_copy(it, off).wait_recv()
        total = ty[it, 0]
        for b in range(1, nz):
            total = total + ty[it, b]
        z_all[it, gx, z_rows(half)] = total
        for off in far_first(nchip):
            z_copy(it, off).start()
        for off in range(1, nz):
            c_copy(it, off).wait_recv()
        part = rows_dot(rblk_s[...], c_all[it].reshape(width, -1))
        rp_send[it] = part.reshape(rp_send.shape[1:])
        rp_all[it, gy] = rp_send[it, gy]
        for off in far_first(ny):
            rp_copy(it, off).start()
        for f in (6, 7, 0, 1, 2, 3, 4, 5):
            on_faces((f,), lambda f: halo_copy(it, f ^ 1).wait_recv())
            whole = prod[it, f] + halo[it, f] if f < 6 else prod[it, f]
            old = start_v[f].astype(F32) if it == 0 else sol[f]
            scale = jnp.concatenate([wb[f]] * (old.shape[1] // block), axis=1)
            sol[f] = old + scale * (loads_v[f].astype(F32) - whole)
        for off in range(1, ny):
            rp_copy(it, off).wait_recv()
        region = rp_all[it, 0]
        for a in range(1, ny):
            region = region + rp_all[it, a]
        depth = modes_t.shape[1]
        sol[...] = sol[...] + dot(modes_t[...], deep_right(region, depth)).reshape(sol.shape)
        if it == ITERS - 1:
            base_out = pltpu.make_async_copy(sol, base_o, out_sem.at[1])
            base_out.start()
        for off in range(1, nchip):
            z_copy(it, off).wait_recv()
        stack = z_all[it].reshape(nx * z_all.shape[2], -1)
        both = rows_dot(rinv_s[...], stack)
        rm = both.shape[0] // 2
        f_send[it, 0] = both[:rm]
        f_send[it, 1] = both[rm:]
        for other, off in finals:
            f_copy(it, other, off).start()
        f_all[it, core, gy] = both[:rm]
        for other, off in finals:
            f_copy(it, other, off).wait_recv()
        root = jnp.concatenate([
            (f_all[it, 0, k] + f_all[it, 1, k]) + (f_all[it, 0, 2 + k] + f_all[it, 1, 2 + k])
            for k in range(2)
        ], axis=1)
        if it < ITERS - 1:
            depth = g_t.shape[1]
            new = sol[...] + dot(g_t[...], deep_right(root, depth)).reshape(sol.shape)
            sol[...] = new
            solb[...] = new.astype(BF16)
        else:
            root_v[...] = root

    root_out = pltpu.make_async_copy(root_v, root_o, out_sem.at[2])
    root_out.start()
    on_faces(range(6), lambda f: modes_copy(f).wait_send())
    for it in range(ITERS):
        on_faces(range(6), lambda f: halo_copy(it, f).wait_send())
        on_faces(range(6), lambda f: kb_copy(it, f).wait_send())
        for off in range(1, nz):
            y_copy(it, off).wait_send()
            c_copy(it, off).wait_send()
        for off in range(1, ny):
            t_copy(it, off).wait_send()
            rp_copy(it, off).wait_send()
        for off in range(1, nchip):
            z_copy(it, off).wait_send()
        for other, off in finals:
            f_copy(it, other, off).wait_send()
    for off in range(1, ny):
        r_copy(off).wait_send()
    root_copy.wait_send()
    g_out.wait()
    base_out.wait()
    root_out.wait()


def last_update(base_h, g_h, root_h, out_h, base, g, root, out, sem, out_sem):
    steps = base.shape[0]
    copies = [
        pltpu.make_async_copy(root_h, root, sem.at[0]),
        pltpu.make_async_copy(g_h, g, sem.at[1]),
    ] + [pltpu.make_async_copy(base_h.at[i], base.at[i], sem.at[2 + i]) for i in range(steps)]
    for copy in copies:
        copy.start()
    copies[0].wait()
    copies[1].wait()
    right = deep_right(root[...], g.shape[-1])
    sent = []
    for i in range(steps):
        copies[2 + i].wait()
        out[i] = base[i] + dot(g[i], right)
        sent.append(pltpu.make_async_copy(out.at[i], out_h.at[i], out_sem.at[i]))
        sent[-1].start()
    for copy in sent:
        copy.wait()


def per_device(
    nx, ny, nz, loads, start, interface_op, block_order, interface_weights, coarse_modes,
    region_weights, region_inverse, root_inverse,
):
    iface, cases = loads.shape[-2:]
    block = iface // 8
    modes_n, rm = region_weights.shape[-2:]
    nchip = nx // 2
    width = nz * modes_n
    faces = (8, block, cases)
    deep_m, deep_g = pad_to(6 * modes_n, 128), pad_to(6 * rm, 128)
    any_spec = pl.BlockSpec(memory_space=pltpu.HBM)
    dma = pltpu.SemaphoreType.DMA
    base, g, root = pl.pallas_call(
        functools.partial(kernel, nx, ny, nz),
        out_shape=(
            jax.ShapeDtypeStruct(faces, F32),
            jax.ShapeDtypeStruct((iface, deep_g), BF16),
            jax.ShapeDtypeStruct((rm, cases), F32),
        ),
        in_specs=[pl.BlockSpec(memory_space=pltpu.SMEM)] + [any_spec] * 8,
        out_specs=(any_spec,) * 3,
        scratch_shapes=[
            pltpu.VMEM(faces, BF16),
            pltpu.VMEM(faces, BF16),
            pltpu.VMEM((8, block, iface), BF16),
            pltpu.VMEM((8, block), F32),
            pltpu.VMEM((modes_n, iface), F32),
            pltpu.VMEM((rm, modes_n), F32),
            pltpu.VMEM((iface, cases), BF16),
            pltpu.VMEM((ITERS, *faces), F32),
            pltpu.VMEM((ITERS, 6, block, cases), F32),
            pltpu.VMEM(faces, F32),
            pltpu.VMEM(faces, BF16),
            pltpu.VMEM((8, block, block), F32),
            pltpu.VMEM((4, 9 * modes_n, 2 * block), BF16),
            pltpu.VMEM((iface, deep_m), BF16),
            pltpu.VMEM((iface, deep_g), BF16),
            pltpu.VMEM((6, modes_n, block), F32),
            pltpu.VMEM((ny, modes_n, width), F32),
            pltpu.VMEM((3 * ny * modes_n, width), BF16),
            pltpu.VMEM((2, rm, nx * rm), F32),
            pltpu.VMEM((6 * rm, nx * rm), BF16),
            pltpu.VMEM((ITERS, 6, modes_n, cases), F32),
            pltpu.VMEM((ITERS, 6, modes_n, cases), F32),
            pltpu.VMEM((ITERS, 4, rm // 2, cases // 2), F32),
            pltpu.VMEM((ITERS, ny, rm // 2, cases // 2), F32),
            pltpu.VMEM((ITERS, nz, rm // 2, cases // 2), F32),
            pltpu.VMEM((ITERS, nz, modes_n, cases), F32),
            pltpu.VMEM((ITERS, ny, modes_n, cases), F32),
            pltpu.VMEM((ITERS, ny, modes_n, cases), F32),
            pltpu.VMEM((ITERS, nx, rm, cases // 2), F32),
            pltpu.VMEM((ITERS, 2, rm, cases // 2), F32),
            pltpu.VMEM((ITERS, 2, ny, rm, cases // 2), F32),
            pltpu.VMEM((rm, cases), F32),
            dma((8,)),
            dma((ITERS, 6)), dma((ITERS, 6)),
            dma((6,)), dma((6,)),
            dma((ITERS, 6)), dma((ITERS, 6)),
            dma((ITERS, ny)), dma((ITERS, ny)),
            dma((ITERS, nz)), dma((ITERS, nz)),
            dma((ITERS, nz)), dma((ITERS, nz)),
            dma((ITERS, nchip)), dma((ITERS, nchip)),
            dma((ny,)), dma((ny,)),
            dma((ITERS, ny)), dma((ITERS, ny)),
            dma((ITERS, 2, ny)), dma((ITERS, 2, ny)),
            dma(()), dma(()),
            dma((3,)),
        ],
        compiler_params=pltpu.CompilerParams(
            collective_id=0, has_side_effects=True, vmem_limit_bytes=67043328
        ),
        name="iterate",
    )(
        block_order.reshape(8),
        loads.reshape(faces),
        start.reshape(faces),
        interface_op.reshape(8, block, iface),
        interface_weights.reshape(8, block),
        coarse_modes.reshape(modes_n, iface),
        region_weights.reshape(modes_n, rm).T,
        region_inverse.reshape(modes_n, -1),
        root_inverse,
    )
    steps = 4
    rows = (steps, iface // steps)
    out = pl.pallas_call(
        last_update,
        out_shape=jax.ShapeDtypeStruct((*rows, cases), F32),
        in_specs=[any_spec] * 3,
        out_specs=any_spec,
        scratch_shapes=[
            pltpu.VMEM((*rows, cases), F32),
            pltpu.VMEM((*rows, deep_g), BF16),
            pltpu.VMEM((rm, cases), F32),
            pltpu.VMEM((*rows, cases), F32),
            dma((2 + steps,)),
            dma((steps,)),
        ],
        compiler_params=pltpu.CompilerParams(vmem_limit_bytes=67043328),
        name="last_update",
    )(base.reshape(*rows, cases), g.reshape(*rows, deep_g), root)
    return out.reshape(1, 1, 1, iface, cases)


def solution(mesh):
    nx, ny, nz = (mesh.shape[axis] for axis in ("gx", "gy", "gz"))
    placed = (
        P("gx", "gy", "gz", None, None),
        P("gx", "gy", "gz", None, None),
        P("gx", "gy", "gz", None, None),
        P("gx", "gy", "gz", None),
        P("gx", "gy", "gz", None),
        P("gx", "gy", "gz", None, None),
        P("gx", "gy", "gz", None, None),
        P("gx", ("gy", "gz"), None),
        P("gx", None),
    )
    return jax.shard_map(
        functools.partial(per_device, nx, ny, nz),
        mesh=mesh,
        in_specs=placed,
        out_specs=P("gx", "gy", "gz", None, None),
        check_vma=False,
    )
```

```python
import functools

import jax
import jax.numpy as jnp
from jax import lax
from jax.experimental import pallas as pl
from jax.experimental.pallas import tpu as pltpu
from jax.sharding import PartitionSpec as P

ITERS = 2
MESH = pl.DeviceIdType.MESH
F32 = jnp.float32
BF16 = jnp.bfloat16
HIGH = lax.Precision.HIGHEST
PAIRS = ((2, 3), (4, 5), (0, 1), (6, 7))
FACES = tuple(f for pair in PAIRS for f in pair)


def dot(a, b):
    return jnp.dot(a, b, preferred_element_type=F32)


def split3(x):
    high = x.astype(BF16)
    rest = x - high.astype(F32)
    mid = rest.astype(BF16)
    low = (rest - mid.astype(F32)).astype(BF16)
    return high, mid, low


def split_rows(x):
    return jnp.concatenate([t.astype(F32) for t in split3(x)], axis=0).astype(BF16)


def rows_dot(left, right):
    n = left.shape[0] // 3
    high, mid, low = split3(right)
    p = dot(left, high)
    q = dot(left[: 2 * n], mid)
    r = dot(left[:n], low)
    return ((r + q[n:]) + p[2 * n :]) + (q[:n] + p[n : 2 * n]) + p[:n]


def deep_left(x, depth):
    high, mid, low = (t.astype(F32) for t in split3(x))
    terms = [high, high, mid, high, mid, low]
    fill = depth - 6 * x.shape[0]
    if fill:
        terms.append(jnp.zeros((fill, x.shape[1]), F32))
    return jnp.concatenate(terms, axis=0).T.astype(BF16)


def deep_right(x, depth):
    high, mid, low = split3(x)
    terms = [high, mid, high, low, mid, high]
    fill = depth - 6 * x.shape[0]
    if fill:
        terms.append(jnp.zeros((fill, x.shape[1]), BF16))
    return jnp.concatenate(terms, axis=0)


def pad_to(n, m):
    return -(-n // m) * m


def kernel(
    nx, ny, nz,
    perm_h, loads_h, start_h, op_h, w_h, modes_h, rw_h, rinv_h, root_h,
    base_o, g_o, root_o,
    perm_s, loads_v, start_v, op_v, op_f, w_v, modes_v, rw_v,
    local, prod, halo, sol, solb, res, wb, modes_s, pair_s, modes_t, g_t, nbm,
    rblk, rblk_s, rinv2, rinv_s, kb_send, kb,
    t_all, c_all, s_all, rp_send, rp_all, z_all, p_send, p_recv,
    in_sem, hs, hr, ns, nr, ks, kr, ts, tr, cs, cr, ss, sr, zs, zr, rs, rr, ps, pr, ms, mr, xs, xr,
):
    gx, gy, gz = lax.axis_index("gx"), lax.axis_index("gy"), lax.axis_index("gz")
    nchip = nx // 2
    chip, core = gx // 2, lax.rem(gx, 2)
    modes_n, iface = modes_v.shape
    block = iface // 8
    width = nz * modes_n
    mate = (gx + 1 - 2 * core, gy, gz)
    beside = (lax.rem(gx + 2 * core - 1 + nx, nx), gy, gz)

    def along_z(off):
        return (gx, gy, lax.rem(gz + off, nz))

    def along_y(off):
        return (gx, lax.rem(gy + off, ny), gz)

    def along_x(off):
        return (lax.rem(chip + off, nchip) * 2 + core, gy, gz)

    def far_first(n):
        return sorted(range(1, n), key=lambda o: -min(o, n - o))

    def remote(src, dst, send, recv, device):
        return pltpu.make_async_remote_copy(
            src_ref=src, dst_ref=dst, send_sem=send, recv_sem=recv,
            device_id=device, device_id_type=MESH,
        )

    def columns(a):
        return pl.ds(pl.multiple_of(a * width, 128), width)

    loaded = {}
    for i, (name, src, dst) in enumerate((
        ("perm", perm_h, perm_s), ("start", start_h, start_v), ("op", op_h, op_v), ("modes", modes_h, modes_v), ("rw", rw_h, rw_v),
        ("loads", loads_h, loads_v), ("w", w_h, w_v), ("root", root_h, rinv2.at[0]),
        ("rinv", rinv_h.at[:, columns(gy)], rblk.at[gy]),
    )):
        loaded[name] = pltpu.make_async_copy(src, dst, in_sem.at[i])
        loaded[name].start()

    barrier = pltpu.get_barrier_semaphore()
    greeted = (
        [along_x(o) for o in far_first(nchip)] + [along_z(o) for o in far_first(nz)]
        + [along_y(o) for o in far_first(ny)] + [beside, mate]
    )
    for device in greeted:
        pl.semaphore_signal(barrier, inc=1, device_id=device, device_id_type=MESH)

    has = (gx > 0, gx < nx - 1, gy > 0, gy < ny - 1, gz > 0, gz < nz - 1)
    towards = (
        (lax.rem(gx + nx - 1, nx), gy, gz), (lax.rem(gx + 1, nx), gy, gz),
        along_y(ny - 1), along_y(1), along_z(nz - 1), along_z(1),
    )

    def halo_copy(it, f):
        return remote(
            prod.at[it, f], halo.at[it, f ^ 1], hs.at[it, f], hr.at[it, f ^ 1], towards[f]
        )

    for f in range(6):

        @pl.when(jnp.logical_not(has[f]))
        def _(f=f):
            nbm[f] = jnp.zeros_like(nbm[f])
            kb[f] = jnp.zeros_like(kb[f])
            for it in range(ITERS):
                halo[it, f] = jnp.zeros_like(halo[it, f])

    loaded["perm"].wait()
    perm = [perm_s[j] for j in range(8)]
    inverse = []
    for f in range(8):
        at = jnp.int32(0)
        for j in range(8):
            at = jnp.where(perm[j] == f, j, at)
        inverse.append(at)

    def on_faces(faces, action):
        for f in faces:
            if f < 6:

                @pl.when(has[f])
                def _(f=f):
                    action(f)

    def modes_copy(f):
        face = modes_h.at[:, f * block : (f + 1) * block]
        return remote(face, nbm.at[f ^ 1], ns.at[f], nr.at[f ^ 1], towards[f])

    def kb_copy(f):
        return remote(kb_send.at[f], kb.at[f ^ 1], ks.at[f], kr.at[f ^ 1], towards[f])

    def t_copy(it, off):
        return remote(
            t_all.at[it, gz], t_all.at[it, gz], ts.at[it, off], tr.at[it, off], along_z(off)
        )

    def c_copy(it, off):
        return remote(
            c_all.at[it, gz], c_all.at[it, gz], cs.at[it, off], cr.at[it, off], along_z(off)
        )

    def s_copy(it, off):
        return remote(
            s_all.at[it, gy], s_all.at[it, gy], ss.at[it, off], sr.at[it, off], along_y(off)
        )

    def z_copy(it, off):
        return remote(
            z_all.at[it, gx], z_all.at[it, gx], zs.at[it, off], zr.at[it, off], along_x(off)
        )

    def r_copy(off):
        to = along_y(off)
        return remote(rinv_h.at[:, columns(to[1])], rblk.at[gy], rs.at[off], rr.at[off], to)

    def rp_copy(it, off):
        to = along_y(off)
        return remote(
            rp_send.at[it, to[1]], rp_all.at[it, gy], ps.at[it, off], pr.at[it, off], to
        )

    def m_copy(it):
        return remote(p_send.at[it], p_recv.at[it], ms.at[it], mr.at[it], mate)

    root_copy = remote(root_h, rinv2.at[1], xs, xr, mate)

    n = modes_n
    loads_c = None
    for it in range(ITERS):
        if it == 0:
            loaded["start"].wait()
            for j in range(8):
                local[j * block : (j + 1) * block, :] = start_v[perm[j]]
            loaded["op"].wait()
            right = local[...]
            for f in FACES:
                prod[it, f] = dot(op_v[inverse[f]], right)
            pl.semaphore_wait(barrier, len(greeted))
            on_faces(FACES, lambda f: halo_copy(it, f).start())
            on_faces(range(6), lambda f: modes_copy(f).start())
            root_copy.start()
            for off in range(1, ny):
                r_copy(off).start()
            loaded["modes"].wait()
            loaded["loads"].wait()
            loaded["rw"].wait()
            modes_s[...] = split_rows(modes_v[...])
            modes_t[...] = deep_left(modes_v[...], modes_t.shape[1])
            g = jnp.dot(rw_v[...], modes_v[...], precision=HIGH, preferred_element_type=F32)
            g_t[...] = deep_left(g, g_t.shape[1])
            loaded["w"].wait()
            for f in range(8):
                wb[f] = jnp.broadcast_to(w_v[f : f + 1, :], (block, block)).T
            for k in range(nchip):
                for i in range(ITERS):
                    z_all[i, 2 * k + 1 - core] = jnp.zeros(z_all.shape[2:], F32)
            coarse = None
            for pair in (PAIRS[3], PAIRS[2], PAIRS[0], PAIRS[1]):
                for f in pair:
                    on_faces((f,), lambda f: halo_copy(it, f ^ 1).wait_recv())
                    whole = prod[it, f] + halo[it, f] if f < 6 else prod[it, f]
                    res[f] = loads_v[f].astype(F32) - whole
                f = pair[0]
                part = rows_dot(
                    modes_s[:, f * block : (f + 2) * block], res[f : f + 2].reshape(2 * block, -1)
                )
                coarse = part if coarse is None else coarse + part
        else:
            for j in range(8):
                local[j * block : (j + 1) * block, :] = solb[perm[j]]
            right = local[...]
            own = None
            for p, pair in enumerate(PAIRS):
                rows = op_f[pair[0] * block : (pair[0] + 2) * block, :]
                both = dot(rows, right)
                prod[it, pair[0]] = both[:block]
                prod[it, pair[1]] = both[block:]
                got = rows_dot(pair_s[p, : 3 * n * (3 if pair[0] < 6 else 1)], both)
                if pair[0] < 6:
                    kb_send[pair[0]] = got[n : 2 * n]
                    kb_send[pair[1]] = got[2 * n :]
                    on_faces(pair, lambda f: kb_copy(f).start())
                own = got[:n] if own is None else own + got[:n]
            on_faces((2, 3, 0, 1), lambda f: halo_copy(it, f).start())
            coarse = loads_c - own
            for f in (0, 1, 2, 3, 4, 5):
                on_faces((f,), lambda f: kb_copy(f ^ 1).wait_recv())
                coarse = coarse - kb[f]
        c_all[it, gz] = coarse
        t_all[it, gz] = jnp.dot(
            rw_v[...], coarse, precision=HIGH, preferred_element_type=F32
        )
        for off in far_first(nz):
            t_copy(it, off).start()
        near = sorted({1, nz - 1})
        for off in near:
            t_copy(it, off).wait_recv()
        for off in far_first(nz):
            c_copy(it, off).start()
        if it:
            on_faces((4, 5), lambda f: halo_copy(it, f).start())
        else:
            for off in range(1, ny):
                r_copy(off).wait_recv()
            loaded["rinv"].wait()
            rblk_s[...] = split_rows(rblk[...].reshape(rblk_s.shape[0] // 3, -1))
            root_copy.wait_recv()
            loaded["root"].wait()
            rinv_s[...] = split_rows(rinv2[...].reshape(rinv_s.shape[0] // 3, -1))
        for off in range(1, nz):
            if off not in near:
                t_copy(it, off).wait_recv()
        total = t_all[it, 0]
        for b in range(1, nz):
            total = total + t_all[it, b]
        s_all[it, gy] = total
        for off in far_first(ny):
            s_copy(it, off).start()
        for off in range(1, ny):
            s_copy(it, off).wait_recv()
        total = s_all[it, 0]
        for a in range(1, ny):
            total = total + s_all[it, a]
        z_all[it, gx] = total
        for off in far_first(nchip):
            z_copy(it, off).start()
        for off in range(1, nz):
            c_copy(it, off).wait_recv()
        part = rows_dot(rblk_s[...], c_all[it].reshape(width, -1))
        rp_send[it] = part.reshape(rp_send.shape[1:])
        rp_all[it, gy] = rp_send[it, gy]
        for off in far_first(ny):
            rp_copy(it, off).start()
        for f in (6, 7, 0, 1, 2, 3, 4, 5):
            if it:
                on_faces((f,), lambda f: halo_copy(it, f ^ 1).wait_recv())
                whole = prod[it, f] + halo[it, f] if f < 6 else prod[it, f]
                rest = loads_v[f].astype(F32) - whole
                old = sol[f]
            else:
                rest = res[f]
                old = start_v[f].astype(F32)
            scale = wb[f]
            sol[f] = old + jnp.concatenate([scale] * (old.shape[1] // block), axis=1) * rest
        if it == 0:
            for f in range(8):
                op_f[f * block : (f + 1) * block, :] = op_v[inverse[f]]
            for f in range(8):
                got = dot(modes_s[:, f * block : (f + 1) * block], loads_v[f])
                loads_c = got if loads_c is None else loads_c + got
            loads_c = (loads_c[2 * n :] + loads_c[n : 2 * n]) + loads_c[:n]
            pair_s[3, : 3 * n] = modes_s[:, 6 * block :]
            fill = jnp.zeros((n, block), F32)
            for p in range(3):
                pair = PAIRS[p]
                on_faces(pair, lambda f: modes_copy(f ^ 1).wait_recv())
                pair_s[p] = split_rows(
                    jnp.concatenate([
                        modes_v[:, pair[0] * block : (pair[0] + 2) * block],
                        jnp.concatenate([nbm[pair[0]], fill], axis=1),
                        jnp.concatenate([fill, nbm[pair[1]]], axis=1),
                    ], axis=0)
                )
        for off in range(1, ny):
            rp_copy(it, off).wait_recv()
        region = rp_all[it, 0]
        for a in range(1, ny):
            region = region + rp_all[it, a]
        depth = modes_t.shape[1]
        with_region = sol[...] + dot(modes_t[...], deep_right(region, depth)).reshape(sol.shape)
        if it < ITERS - 1:
            sol[...] = with_region
        else:
            base_o[...] = with_region
            g_o[...] = g_t[...]
        for off in range(1, nchip):
            z_copy(it, off).wait_recv()
        stack = z_all[it].reshape(nx * z_all.shape[2], -1)
        both = rows_dot(rinv_s[...], stack)
        rm = both.shape[0] // 2
        p_send[it] = both[rm:]
        m_copy(it).start()
        m_copy(it).wait_recv()
        root = both[:rm] + p_recv[it]
        if it < ITERS - 1:
            depth = g_t.shape[1]
            new = sol[...] + dot(g_t[...], deep_right(root, depth)).reshape(sol.shape)
            sol[...] = new
            solb[...] = new.astype(BF16)
        else:
            root_o[...] = root

    on_faces(range(6), lambda f: modes_copy(f).wait_send())
    on_faces(range(6), lambda f: kb_copy(f).wait_send())
    for it in range(ITERS):
        on_faces(range(6), lambda f: halo_copy(it, f).wait_send())
        for off in range(1, nz):
            t_copy(it, off).wait_send()
            c_copy(it, off).wait_send()
        for off in range(1, ny):
            s_copy(it, off).wait_send()
            rp_copy(it, off).wait_send()
        for off in range(1, nchip):
            z_copy(it, off).wait_send()
        m_copy(it).wait_send()
    for off in range(1, ny):
        r_copy(off).wait_send()
    root_copy.wait_send()


def last_update(base, g, root, out_h, out, sem):
    right = deep_right(root[...], g.shape[1])
    steps, rows = out.shape[0], out.shape[1]
    sent = []
    for i in range(steps):
        at = slice(i * rows, (i + 1) * rows)
        out[i] = base[at] + dot(g[at], right)
        sent.append(pltpu.make_async_copy(out.at[i], out_h.at[i], sem.at[i]))
        sent[-1].start()
    for copy in sent:
        copy.wait()


def per_device(
    nx, ny, nz, loads, start, interface_op, block_order, interface_weights, coarse_modes,
    region_weights, region_inverse, root_inverse,
):
    iface, cases = loads.shape[-2:]
    block = iface // 8
    modes_n, rm = region_weights.shape[-2:]
    nchip = nx // 2
    width = nz * modes_n
    faces = (8, block, cases)
    deep_m, deep_g = pad_to(6 * modes_n, 128), pad_to(6 * rm, 128)
    hbm_spec = pl.BlockSpec(memory_space=pltpu.HBM)
    vmem_spec = pl.BlockSpec(memory_space=pltpu.VMEM)
    dma = pltpu.SemaphoreType.DMA
    base, g, root = pl.pallas_call(
        functools.partial(kernel, nx, ny, nz),
        out_shape=(
            jax.ShapeDtypeStruct(faces, F32),
            jax.ShapeDtypeStruct((iface, deep_g), BF16),
            jax.ShapeDtypeStruct((rm, cases), F32),
        ),
        in_specs=[hbm_spec] * 9,
        out_specs=(vmem_spec,) * 3,
        scratch_shapes=[
            pltpu.SMEM((8,), jnp.int32),
            pltpu.VMEM(faces, BF16),
            pltpu.VMEM(faces, BF16),
            pltpu.VMEM((8, block, iface), BF16),
            pltpu.VMEM((iface, iface), BF16),
            pltpu.VMEM((8, block), F32),
            pltpu.VMEM((modes_n, iface), F32),
            pltpu.VMEM((rm, modes_n), F32),
            pltpu.VMEM((iface, cases), BF16),
            pltpu.VMEM((ITERS, *faces), F32),
            pltpu.VMEM((ITERS, 6, block, cases), F32),
            pltpu.VMEM(faces, F32),
            pltpu.VMEM(faces, BF16),
            pltpu.VMEM(faces, F32),
            pltpu.VMEM((8, block, block), F32),
            pltpu.VMEM((3 * modes_n, iface), BF16),
            pltpu.VMEM((4, 9 * modes_n, 2 * block), BF16),
            pltpu.VMEM((iface, deep_m), BF16),
            pltpu.VMEM((iface, deep_g), BF16),
            pltpu.VMEM((6, modes_n, block), F32),
            pltpu.VMEM((ny, modes_n, width), F32),
            pltpu.VMEM((3 * ny * modes_n, width), BF16),
            pltpu.VMEM((2, rm, nx * rm), F32),
            pltpu.VMEM((6 * rm, nx * rm), BF16),
            pltpu.VMEM((6, modes_n, cases), F32),
            pltpu.VMEM((6, modes_n, cases), F32),
            pltpu.VMEM((ITERS, nz, rm, cases), F32),
            pltpu.VMEM((ITERS, nz, modes_n, cases), F32),
            pltpu.VMEM((ITERS, ny, rm, cases), F32),
            pltpu.VMEM((ITERS, ny, modes_n, cases), F32),
            pltpu.VMEM((ITERS, ny, modes_n, cases), F32),
            pltpu.VMEM((ITERS, nx, rm, cases), F32),
            pltpu.VMEM((ITERS, rm, cases), F32),
            pltpu.VMEM((ITERS, rm, cases), F32),
            dma((9,)),
            dma((ITERS, 6)), dma((ITERS, 6)),
            dma((6,)), dma((6,)),
            dma((6,)), dma((6,)),
            dma((ITERS, nz)), dma((ITERS, nz)),
            dma((ITERS, nz)), dma((ITERS, nz)),
            dma((ITERS, ny)), dma((ITERS, ny)),
            dma((ITERS, nchip)), dma((ITERS, nchip)),
            dma((ny,)), dma((ny,)),
            dma((ITERS, ny)), dma((ITERS, ny)),
            dma((ITERS,)), dma((ITERS,)),
            dma(()), dma(()),
        ],
        compiler_params=pltpu.CompilerParams(
            collective_id=0, has_side_effects=True, vmem_limit_bytes=44 * 2**20
        ),
        name="iterate",
    )(
        *(
            pltpu.with_memory_space_constraint(x, pltpu.HBM)
            for x in (
                block_order.reshape(8),
                loads.reshape(faces),
                start.reshape(faces),
                interface_op.reshape(8, block, iface),
                interface_weights.reshape(8, block),
                coarse_modes.reshape(modes_n, iface),
                region_weights.reshape(modes_n, rm).T,
                region_inverse.reshape(modes_n, -1),
                root_inverse,
            )
        )
    )
    rows = (4, iface // 4, cases)
    out = pl.pallas_call(
        last_update,
        out_shape=jax.ShapeDtypeStruct(rows, F32),
        in_specs=[vmem_spec] * 3,
        out_specs=hbm_spec,
        scratch_shapes=[pltpu.VMEM(rows, F32), dma((4,))],
        compiler_params=pltpu.CompilerParams(vmem_limit_bytes=16 * 2**20),
        name="last_update",
    )(base.reshape(iface, cases), g, root)
    return out.reshape(1, 1, 1, iface, cases)


def solution(mesh):
    nx, ny, nz = (mesh.shape[axis] for axis in ("gx", "gy", "gz"))
    placed = (
        P("gx", "gy", "gz", None, None),
        P("gx", "gy", "gz", None, None),
        P("gx", "gy", "gz", None, None),
        P("gx", "gy", "gz", None),
        P("gx", "gy", "gz", None),
        P("gx", "gy", "gz", None, None),
        P("gx", "gy", "gz", None, None),
        P("gx", ("gy", "gz"), None),
        P("gx", None),
    )
    return jax.shard_map(
        functools.partial(per_device, nx, ny, nz),
        mesh=mesh,
        in_specs=placed,
        out_specs=P("gx", "gy", "gz", None, None),
        check_vma=False,
    )
```

```python
import functools

import jax
import jax.numpy as jnp
from jax import lax
from jax.experimental import pallas as pl
from jax.experimental.pallas import tpu as pltpu
from jax.sharding import PartitionSpec as P

ITERS = 2
MESH = pl.DeviceIdType.MESH
F32 = jnp.float32
BF16 = jnp.bfloat16
HIGH = lax.Precision.HIGHEST
PAIRS = ((2, 3), (4, 5), (0, 1), (6, 7))
FACES = tuple(f for pair in PAIRS for f in pair)


def dot(a, b):
    return jnp.dot(a, b, preferred_element_type=F32)


def split3(x):
    high = x.astype(BF16)
    rest = x - high.astype(F32)
    mid = rest.astype(BF16)
    low = (rest - mid.astype(F32)).astype(BF16)
    return high, mid, low


def split_rows(x):
    return jnp.concatenate([t.astype(F32) for t in split3(x)], axis=0).astype(BF16)


def rows_dot(left, right):
    n = left.shape[0] // 3
    high, mid, low = split3(right)
    p = dot(left, high)
    q = dot(left[: 2 * n], mid)
    r = dot(left[:n], low)
    return ((r + q[n:]) + p[2 * n :]) + (q[:n] + p[n : 2 * n]) + p[:n]


def deep_left(x, depth):
    high, mid, low = (t.astype(F32) for t in split3(x))
    terms = [high, high, mid, high, mid, low]
    fill = depth - 6 * x.shape[0]
    if fill:
        terms.append(jnp.zeros((fill, x.shape[1]), F32))
    return jnp.concatenate(terms, axis=0).T.astype(BF16)


def deep_right(x, depth):
    high, mid, low = split3(x)
    terms = [high, mid, high, low, mid, high]
    fill = depth - 6 * x.shape[0]
    if fill:
        terms.append(jnp.zeros((fill, x.shape[1]), BF16))
    return jnp.concatenate(terms, axis=0)


def pad_to(n, m):
    return -(-n // m) * m


def kernel(
    nx, ny, nz,
    perm_h, loads_h, start_h, op_h, w_h, modes_h, rw_h, rinv_h, root_h,
    base_o, g_o, root_o,
    perm_s, loads_v, start_v, op_v, op_f, w_v, modes_v, rw_v, rinv_v, r_send,
    local, prod, halo, sol, solb, res, wb, modes_s, pair_s, modes_t, g_t, nbm,
    rblk, rblk_s, rinv2, rinv_s, kb_send, kb,
    t_all, c_all, s_all, rp_send, rp_all, z_all, p_send, p_recv,
    in_sem, hs, hr, ns, nr, ks, kr, ts, tr, cs, cr, ss, sr, zs, zr, rs, rr, ps, pr, ms, mr, xs, xr,
):
    gx, gy, gz = lax.axis_index("gx"), lax.axis_index("gy"), lax.axis_index("gz")
    nchip = nx // 2
    chip, core = gx // 2, lax.rem(gx, 2)
    modes_n, iface = modes_v.shape
    block = iface // 8
    width = nz * modes_n
    mate = (gx + 1 - 2 * core, gy, gz)
    beside = (lax.rem(gx + 2 * core - 1 + nx, nx), gy, gz)

    def along_z(off):
        return (gx, gy, lax.rem(gz + off, nz))

    def along_y(off):
        return (gx, lax.rem(gy + off, ny), gz)

    def along_x(off):
        return (lax.rem(chip + off, nchip) * 2 + core, gy, gz)

    def far_first(n):
        return sorted(range(1, n), key=lambda o: -min(o, n - o))

    def remote(src, dst, send, recv, device):
        return pltpu.make_async_remote_copy(
            src_ref=src, dst_ref=dst, send_sem=send, recv_sem=recv,
            device_id=device, device_id_type=MESH,
        )

    loaded = {}
    for i, (name, src, dst) in enumerate((
        ("perm", perm_h, perm_s), ("start", start_h, start_v), ("op", op_h, op_v), ("modes", modes_h, modes_v), ("rw", rw_h, rw_v),
        ("loads", loads_h, loads_v), ("w", w_h, w_v), ("root", root_h, rinv2.at[0]),
        ("rinv", rinv_h, rinv_v),
    )):
        loaded[name] = pltpu.make_async_copy(src, dst, in_sem.at[i])
        loaded[name].start()

    barrier = pltpu.get_barrier_semaphore()
    greeted = (
        [along_x(o) for o in far_first(nchip)] + [along_z(o) for o in far_first(nz)]
        + [along_y(o) for o in far_first(ny)] + [beside, mate]
    )
    for device in greeted:
        pl.semaphore_signal(barrier, inc=1, device_id=device, device_id_type=MESH)

    has = (gx > 0, gx < nx - 1, gy > 0, gy < ny - 1, gz > 0, gz < nz - 1)
    towards = (
        (lax.rem(gx + nx - 1, nx), gy, gz), (lax.rem(gx + 1, nx), gy, gz),
        along_y(ny - 1), along_y(1), along_z(nz - 1), along_z(1),
    )

    def halo_copy(it, f):
        return remote(
            prod.at[it, f], halo.at[it, f ^ 1], hs.at[it, f], hr.at[it, f ^ 1], towards[f]
        )

    for f in range(6):

        @pl.when(jnp.logical_not(has[f]))
        def _(f=f):
            nbm[f] = jnp.zeros_like(nbm[f])
            kb[f] = jnp.zeros_like(kb[f])
            for it in range(ITERS):
                halo[it, f] = jnp.zeros_like(halo[it, f])

    loaded["perm"].wait()
    perm = [perm_s[j] for j in range(8)]
    inverse = []
    for f in range(8):
        at = jnp.int32(0)
        for j in range(8):
            at = jnp.where(perm[j] == f, j, at)
        inverse.append(at)

    def on_faces(faces, action):
        for f in faces:
            if f < 6:

                @pl.when(has[f])
                def _(f=f):
                    action(f)

    def modes_copy(f):
        face = modes_h.at[:, f * block : (f + 1) * block]
        return remote(face, nbm.at[f ^ 1], ns.at[f], nr.at[f ^ 1], towards[f])

    def kb_copy(f):
        return remote(kb_send.at[f], kb.at[f ^ 1], ks.at[f], kr.at[f ^ 1], towards[f])

    def t_copy(it, off):
        return remote(
            t_all.at[it, gz], t_all.at[it, gz], ts.at[it, off], tr.at[it, off], along_z(off)
        )

    def c_copy(it, off):
        return remote(
            c_all.at[it, gy], c_all.at[it, gy], cs.at[it, off], cr.at[it, off], along_y(off)
        )

    def s_copy(it, off):
        return remote(
            s_all.at[it, gy], s_all.at[it, gy], ss.at[it, off], sr.at[it, off], along_y(off)
        )

    def z_copy(it, off):
        return remote(
            z_all.at[it, gx], z_all.at[it, gx], zs.at[it, off], zr.at[it, off], along_x(off)
        )

    def r_copy(off):
        to = along_z(off)
        return remote(r_send.at[to[2]], rblk.at[gz], rs.at[off], rr.at[off], to)

    def rp_copy(it, off):
        to = along_z(off)
        return remote(
            rp_send.at[it, to[2]], rp_all.at[it, gz], ps.at[it, off], pr.at[it, off], to
        )

    def m_copy(it):
        return remote(p_send.at[it], p_recv.at[it], ms.at[it], mr.at[it], mate)

    root_copy = remote(root_h, rinv2.at[1], xs, xr, mate)

    n = modes_n
    loads_c = None
    for it in range(ITERS):
        if it == 0:
            loaded["start"].wait()
            for j in range(8):
                local[j * block : (j + 1) * block, :] = start_v[perm[j]]
            loaded["op"].wait()
            right = local[...]
            for f in FACES:
                prod[it, f] = dot(op_v[inverse[f]], right)
            pl.semaphore_wait(barrier, len(greeted))
            on_faces(FACES, lambda f: halo_copy(it, f).start())
            on_faces(range(6), lambda f: modes_copy(f).start())
            root_copy.start()
            loaded["rinv"].wait()
            for b in range(nz):
                r_send[b] = jnp.concatenate(
                    [
                        rinv_v[:, a * width + b * n : a * width + (b + 1) * n]
                        for a in range(ny)
                    ],
                    axis=1,
                )
            for off in far_first(nz):
                r_copy(off).start()
            rblk[gz] = r_send[gz]
            loaded["modes"].wait()
            loaded["loads"].wait()
            loaded["rw"].wait()
            modes_s[...] = split_rows(modes_v[...])
            modes_t[...] = deep_left(modes_v[...], modes_t.shape[1])
            g = jnp.dot(rw_v[...], modes_v[...], precision=HIGH, preferred_element_type=F32)
            g_t[...] = deep_left(g, g_t.shape[1])
            loaded["w"].wait()
            for f in range(8):
                wb[f] = jnp.broadcast_to(w_v[f : f + 1, :], (block, block)).T
            for k in range(nchip):
                for i in range(ITERS):
                    z_all[i, 2 * k + 1 - core] = jnp.zeros(z_all.shape[2:], F32)
            coarse = None
            for pair in (PAIRS[3], PAIRS[2], PAIRS[0], PAIRS[1]):
                for f in pair:
                    on_faces((f,), lambda f: halo_copy(it, f ^ 1).wait_recv())
                    whole = prod[it, f] + halo[it, f] if f < 6 else prod[it, f]
                    res[f] = loads_v[f].astype(F32) - whole
                f = pair[0]
                part = rows_dot(
                    modes_s[:, f * block : (f + 2) * block], res[f : f + 2].reshape(2 * block, -1)
                )
                coarse = part if coarse is None else coarse + part
        else:
            for j in range(8):
                local[j * block : (j + 1) * block, :] = solb[perm[j]]
            right = local[...]
            own = None
            for p, pair in enumerate(PAIRS):
                rows = op_f[pair[0] * block : (pair[0] + 2) * block, :]
                both = dot(rows, right)
                prod[it, pair[0]] = both[:block]
                prod[it, pair[1]] = both[block:]
                got = rows_dot(pair_s[p, : 3 * n * (3 if pair[0] < 6 else 1)], both)
                if pair[0] < 6:
                    kb_send[pair[0]] = got[n : 2 * n]
                    kb_send[pair[1]] = got[2 * n :]
                    on_faces(pair, lambda f: kb_copy(f).start())
                own = got[:n] if own is None else own + got[:n]
            on_faces((0, 1), lambda f: halo_copy(it, f).start())
            coarse = loads_c - own
            for f in (0, 1, 2, 3, 4, 5):
                on_faces((f,), lambda f: kb_copy(f ^ 1).wait_recv())
                coarse = coarse - kb[f]
        c_all[it, gy] = coarse
        t_all[it, gz] = jnp.dot(
            rw_v[...], coarse, precision=HIGH, preferred_element_type=F32
        )
        for off in far_first(nz):
            t_copy(it, off).start()
        for off in far_first(ny):
            c_copy(it, off).start()
        if it:
            on_faces((2, 3), lambda f: halo_copy(it, f).start())
        else:
            for off in range(1, nz):
                r_copy(off).wait_recv()
            rblk_s[...] = split_rows(rblk[...].reshape(rblk_s.shape[0] // 3, -1))
            root_copy.wait_recv()
            loaded["root"].wait()
            rinv_s[...] = split_rows(rinv2[...].reshape(rinv_s.shape[0] // 3, -1))
        for off in range(1, ny):
            c_copy(it, off).wait_recv()
        part = rows_dot(rblk_s[...], c_all[it].reshape(ny * n, -1))
        rp_send[it] = part.reshape(rp_send.shape[1:])
        for off in range(1, nz):
            t_copy(it, off).wait_recv()
        total = t_all[it, 0]
        for b in range(1, nz):
            total = total + t_all[it, b]
        s_all[it, gy] = total
        for off in far_first(ny):
            s_copy(it, off).start()
        for off in far_first(nz):
            rp_copy(it, off).start()
        rp_all[it, gz] = rp_send[it, gz]
        if it:
            on_faces((4, 5), lambda f: halo_copy(it, f).start())
        for off in range(1, ny):
            s_copy(it, off).wait_recv()
        total = s_all[it, 0]
        for a in range(1, ny):
            total = total + s_all[it, a]
        z_all[it, gx] = total
        for off in far_first(nchip):
            z_copy(it, off).start()
        for f in (6, 7, 0, 1, 2, 3, 4, 5):
            if it:
                on_faces((f,), lambda f: halo_copy(it, f ^ 1).wait_recv())
                whole = prod[it, f] + halo[it, f] if f < 6 else prod[it, f]
                rest = loads_v[f].astype(F32) - whole
                old = sol[f]
            else:
                rest = res[f]
                old = start_v[f].astype(F32)
            scale = wb[f]
            sol[f] = old + jnp.concatenate([scale] * (old.shape[1] // block), axis=1) * rest
        if it == 0:
            for f in range(8):
                op_f[f * block : (f + 1) * block, :] = op_v[inverse[f]]
            for f in range(8):
                got = dot(modes_s[:, f * block : (f + 1) * block], loads_v[f])
                loads_c = got if loads_c is None else loads_c + got
            loads_c = (loads_c[2 * n :] + loads_c[n : 2 * n]) + loads_c[:n]
            pair_s[3, : 3 * n] = modes_s[:, 6 * block :]
            fill = jnp.zeros((n, block), F32)
            for p in range(3):
                pair = PAIRS[p]
                on_faces(pair, lambda f: modes_copy(f ^ 1).wait_recv())
                pair_s[p] = split_rows(
                    jnp.concatenate([
                        modes_v[:, pair[0] * block : (pair[0] + 2) * block],
                        jnp.concatenate([nbm[pair[0]], fill], axis=1),
                        jnp.concatenate([fill, nbm[pair[1]]], axis=1),
                    ], axis=0)
                )
        for off in range(1, nz):
            rp_copy(it, off).wait_recv()
        region = rp_all[it, 0]
        for b in range(1, nz):
            region = region + rp_all[it, b]
        depth = modes_t.shape[1]
        with_region = sol[...] + dot(modes_t[...], deep_right(region, depth)).reshape(sol.shape)
        if it < ITERS - 1:
            sol[...] = with_region
        else:
            base_o[...] = with_region
            g_o[...] = g_t[...]
        for off in range(1, nchip):
            z_copy(it, off).wait_recv()
        stack = z_all[it].reshape(nx * z_all.shape[2], -1)
        both = rows_dot(rinv_s[...], stack)
        rm = both.shape[0] // 2
        p_send[it] = both[rm:]
        m_copy(it).start()
        m_copy(it).wait_recv()
        root = both[:rm] + p_recv[it]
        if it < ITERS - 1:
            depth = g_t.shape[1]
            new = sol[...] + dot(g_t[...], deep_right(root, depth)).reshape(sol.shape)
            sol[...] = new
            solb[...] = new.astype(BF16)
        else:
            root_o[...] = root

    on_faces(range(6), lambda f: modes_copy(f).wait_send())
    on_faces(range(6), lambda f: kb_copy(f).wait_send())
    for it in range(ITERS):
        on_faces(range(6), lambda f: halo_copy(it, f).wait_send())
        for off in range(1, nz):
            t_copy(it, off).wait_send()
            rp_copy(it, off).wait_send()
        for off in range(1, ny):
            s_copy(it, off).wait_send()
            c_copy(it, off).wait_send()
        for off in range(1, nchip):
            z_copy(it, off).wait_send()
        m_copy(it).wait_send()
    for off in range(1, nz):
        r_copy(off).wait_send()
    root_copy.wait_send()


def last_update(base, g, root, out_h, out, sem):
    right = deep_right(root[...], g.shape[1])
    steps, rows = out.shape[0], out.shape[1]
    sent = []
    for i in range(steps):
        at = slice(i * rows, (i + 1) * rows)
        out[i] = base[at] + dot(g[at], right)
        sent.append(pltpu.make_async_copy(out.at[i], out_h.at[i], sem.at[i]))
        sent[-1].start()
    for copy in sent:
        copy.wait()


def per_device(
    nx, ny, nz, loads, start, interface_op, block_order, interface_weights, coarse_modes,
    region_weights, region_inverse, root_inverse,
):
    iface, cases = loads.shape[-2:]
    block = iface // 8
    modes_n, rm = region_weights.shape[-2:]
    nchip = nx // 2
    width = nz * modes_n
    faces = (8, block, cases)
    deep_m, deep_g = pad_to(6 * modes_n, 128), pad_to(6 * rm, 128)
    hbm_spec = pl.BlockSpec(memory_space=pltpu.HBM)
    vmem_spec = pl.BlockSpec(memory_space=pltpu.VMEM)
    dma = pltpu.SemaphoreType.DMA
    base, g, root = pl.pallas_call(
        functools.partial(kernel, nx, ny, nz),
        out_shape=(
            jax.ShapeDtypeStruct(faces, F32),
            jax.ShapeDtypeStruct((iface, deep_g), BF16),
            jax.ShapeDtypeStruct((rm, cases), F32),
        ),
        in_specs=[hbm_spec] * 9,
        out_specs=(vmem_spec,) * 3,
        scratch_shapes=[
            pltpu.SMEM((8,), jnp.int32),
            pltpu.VMEM(faces, BF16),
            pltpu.VMEM(faces, BF16),
            pltpu.VMEM((8, block, iface), BF16),
            pltpu.VMEM((iface, iface), BF16),
            pltpu.VMEM((8, block), F32),
            pltpu.VMEM((modes_n, iface), F32),
            pltpu.VMEM((rm, modes_n), F32),
            pltpu.VMEM((modes_n, ny * width), F32),
            pltpu.VMEM((nz, modes_n, ny * modes_n), F32),
            pltpu.VMEM((iface, cases), BF16),
            pltpu.VMEM((ITERS, *faces), F32),
            pltpu.VMEM((ITERS, 6, block, cases), F32),
            pltpu.VMEM(faces, F32),
            pltpu.VMEM(faces, BF16),
            pltpu.VMEM(faces, F32),
            pltpu.VMEM((8, block, block), F32),
            pltpu.VMEM((3 * modes_n, iface), BF16),
            pltpu.VMEM((4, 9 * modes_n, 2 * block), BF16),
            pltpu.VMEM((iface, deep_m), BF16),
            pltpu.VMEM((iface, deep_g), BF16),
            pltpu.VMEM((6, modes_n, block), F32),
            pltpu.VMEM((nz, modes_n, ny * modes_n), F32),
            pltpu.VMEM((3 * width, ny * modes_n), BF16),
            pltpu.VMEM((2, rm, nx * rm), F32),
            pltpu.VMEM((6 * rm, nx * rm), BF16),
            pltpu.VMEM((6, modes_n, cases), F32),
            pltpu.VMEM((6, modes_n, cases), F32),
            pltpu.VMEM((ITERS, nz, rm, cases), F32),
            pltpu.VMEM((ITERS, ny, modes_n, cases), F32),
            pltpu.VMEM((ITERS, ny, rm, cases), F32),
            pltpu.VMEM((ITERS, nz, modes_n, cases), F32),
            pltpu.VMEM((ITERS, nz, modes_n, cases), F32),
            pltpu.VMEM((ITERS, nx, rm, cases), F32),
            pltpu.VMEM((ITERS, rm, cases), F32),
            pltpu.VMEM((ITERS, rm, cases), F32),
            dma((9,)),
            dma((ITERS, 6)), dma((ITERS, 6)),
            dma((6,)), dma((6,)),
            dma((6,)), dma((6,)),
            dma((ITERS, nz)), dma((ITERS, nz)),
            dma((ITERS, ny)), dma((ITERS, ny)),
            dma((ITERS, ny)), dma((ITERS, ny)),
            dma((ITERS, nchip)), dma((ITERS, nchip)),
            dma((nz,)), dma((nz,)),
            dma((ITERS, nz)), dma((ITERS, nz)),
            dma((ITERS,)), dma((ITERS,)),
            dma(()), dma(()),
        ],
        compiler_params=pltpu.CompilerParams(
            collective_id=0, has_side_effects=True, vmem_limit_bytes=44 * 2**20
        ),
        name="iterate",
    )(
        *(
            pltpu.with_memory_space_constraint(x, pltpu.HBM)
            for x in (
                block_order.reshape(8),
                loads.reshape(faces),
                start.reshape(faces),
                interface_op.reshape(8, block, iface),
                interface_weights.reshape(8, block),
                coarse_modes.reshape(modes_n, iface),
                region_weights.reshape(modes_n, rm).T,
                region_inverse.reshape(modes_n, -1),
                root_inverse,
            )
        )
    )
    rows = (4, iface // 4, cases)
    out = pl.pallas_call(
        last_update,
        out_shape=jax.ShapeDtypeStruct(rows, F32),
        in_specs=[vmem_spec] * 3,
        out_specs=hbm_spec,
        scratch_shapes=[pltpu.VMEM(rows, F32), dma((4,))],
        compiler_params=pltpu.CompilerParams(vmem_limit_bytes=16 * 2**20),
        name="last_update",
    )(base.reshape(iface, cases), g, root)
    return out.reshape(1, 1, 1, iface, cases)


def solution(mesh):
    nx, ny, nz = (mesh.shape[axis] for axis in ("gx", "gy", "gz"))
    placed = (
        P("gx", "gy", "gz", None, None),
        P("gx", "gy", "gz", None, None),
        P("gx", "gy", "gz", None, None),
        P("gx", "gy", "gz", None),
        P("gx", "gy", "gz", None),
        P("gx", "gy", "gz", None, None),
        P("gx", "gy", "gz", None, None),
        P("gx", ("gy", "gz"), None),
        P("gx", None),
    )
    return jax.shard_map(
        functools.partial(per_device, nx, ny, nz),
        mesh=mesh,
        in_specs=placed,
        out_specs=P("gx", "gy", "gz", None, None),
        check_vma=False,
    )
```

```python
import functools

import jax
import jax.numpy as jnp
from jax import lax
from jax.experimental import pallas as pl
from jax.experimental.pallas import tpu as pltpu
from jax.sharding import PartitionSpec as P

ITERS = 2
MESH = pl.DeviceIdType.MESH
F32 = jnp.float32
BF16 = jnp.bfloat16
HIGH = lax.Precision.HIGHEST
PAIRS = ((2, 3), (4, 5), (0, 1), (6, 7))
FACES = tuple(f for pair in PAIRS for f in pair)


def dot(a, b):
    return jnp.dot(a, b, preferred_element_type=F32)


def split3(x):
    high = x.astype(BF16)
    rest = x - high.astype(F32)
    mid = rest.astype(BF16)
    low = (rest - mid.astype(F32)).astype(BF16)
    return high, mid, low


def split_rows(x):
    return jnp.concatenate([t.astype(F32) for t in split3(x)], axis=0).astype(BF16)


def rows_dot(left, right):
    n = left.shape[0] // 3
    high, mid, low = split3(right)
    p = dot(left, high)
    q = dot(left[: 2 * n], mid)
    r = dot(left[:n], low)
    return ((r + q[n:]) + p[2 * n :]) + (q[:n] + p[n : 2 * n]) + p[:n]


def rows_dot_last(left, right):
    n = left.shape[0] // 3
    high = right.astype(BF16)
    p = dot(left[: 2 * n], high)
    return (dot(left[:n], (right - high.astype(F32)).astype(BF16)) + p[n:]) + p[:n]


def deep_left(x, depth):
    high, mid, low = (t.astype(F32) for t in split3(x))
    terms = [high, high, mid, high, mid, low]
    fill = depth - 6 * x.shape[0]
    if fill:
        terms.append(jnp.zeros((fill, x.shape[1]), F32))
    return jnp.concatenate(terms, axis=0).T.astype(BF16)


def deep_right(x, depth):
    high, mid, low = split3(x)
    terms = [high, mid, high, low, mid, high]
    fill = depth - 6 * x.shape[0]
    if fill:
        terms.append(jnp.zeros((fill, x.shape[1]), BF16))
    return jnp.concatenate(terms, axis=0)


def pad_to(n, m):
    return -(-n // m) * m


def kernel(
    nx, ny, nz,
    perm_h, loads_h, start_h, op_h, w_h, modes_h, rw_h, rinv_h, root_h,
    base_o, g_o, root_o,
    perm_s, loads_v, start_v, op_v, op_f, w_v, modes_v, rw_v, rinv_v, r_send,
    local, prod, halo, sol, solb, res, wb, modes_s, pair_s, modes_t, g_t, nbm,
    rblk, rblk_s, rinv2, rinv_s, kb_send, kb,
    t_all, c_all, s_all, rp_send, rp_all, z_all, p_send, p_recv,
    in_sem, hs, hr, ns, nr, ks, kr, ts, tr, cs, cr, ss, sr, zs, zr, rs, rr, ps, pr, ms, mr, xs, xr, root_v, out_sem,
):
    gx, gy, gz = lax.axis_index("gx"), lax.axis_index("gy"), lax.axis_index("gz")
    nchip = nx // 2
    chip, core = gx // 2, lax.rem(gx, 2)
    modes_n, iface = modes_v.shape
    block = iface // 8
    width = nz * modes_n
    mate = (gx + 1 - 2 * core, gy, gz)
    beside = (lax.rem(gx + 2 * core - 1 + nx, nx), gy, gz)

    def along_z(off):
        return (gx, gy, lax.rem(gz + off, nz))

    def along_y(off):
        return (gx, lax.rem(gy + off, ny), gz)

    def along_x(off):
        return (lax.rem(chip + off, nchip) * 2 + core, gy, gz)

    def far_first(n):
        return sorted(range(1, n), key=lambda o: -min(o, n - o))

    def remote(src, dst, send, recv, device):
        return pltpu.make_async_remote_copy(
            src_ref=src, dst_ref=dst, send_sem=send, recv_sem=recv,
            device_id=device, device_id_type=MESH,
        )

    barrier = pltpu.get_barrier_semaphore()
    greeted = (
        [along_x(o) for o in far_first(nchip)] + [along_z(o) for o in far_first(nz)]
        + [along_y(o) for o in far_first(ny)] + [beside, mate]
    )
    for device in greeted:
        pl.semaphore_signal(barrier, inc=1, device_id=device, device_id_type=MESH)

    loaded = {}
    for i, (name, src, dst) in enumerate((
        ("perm", perm_h, perm_s), ("start", start_h, start_v), ("op", op_h, op_v), ("modes", modes_h, modes_v), ("rw", rw_h, rw_v),
        ("loads", loads_h, loads_v), ("w", w_h, w_v), ("root", root_h, rinv2.at[0]),
        ("rinv", rinv_h, rinv_v),
    )):
        loaded[name] = pltpu.make_async_copy(src, dst, in_sem.at[i])
        loaded[name].start()

    has = (gx > 0, gx < nx - 1, gy > 0, gy < ny - 1, gz > 0, gz < nz - 1)
    towards = (
        (lax.rem(gx + nx - 1, nx), gy, gz), (lax.rem(gx + 1, nx), gy, gz),
        along_y(ny - 1), along_y(1), along_z(nz - 1), along_z(1),
    )

    def halo_copy(it, f):
        return remote(
            prod.at[it, f], halo.at[it, f ^ 1], hs.at[it, f], hr.at[it, f ^ 1], towards[f]
        )

    loaded["perm"].wait()
    perm = [perm_s[j] for j in range(8)]
    inverse = []
    for f in range(8):
        at = jnp.int32(0)
        for j in range(8):
            at = jnp.where(perm[j] == f, j, at)
        inverse.append(at)

    def on_faces(faces, action):
        for f in faces:
            if f < 6:

                @pl.when(has[f])
                def _(f=f):
                    action(f)

    def modes_copy(f):
        face = modes_h.at[:, f * block : (f + 1) * block]
        return remote(face, nbm.at[f ^ 1], ns.at[f], nr.at[f ^ 1], towards[f])

    def kb_copy(f):
        return remote(kb_send.at[f], kb.at[f ^ 1], ks.at[f], kr.at[f ^ 1], towards[f])

    def t_copy(it, off):
        return remote(
            t_all.at[it, gz], t_all.at[it, gz], ts.at[it], tr.at[it], along_z(off)
        )

    def c_copy(it, off):
        return remote(
            c_all.at[it, gy], c_all.at[it, gy], cs.at[it], cr.at[it], along_y(off)
        )

    def all_of(buffer, count, sem):
        blocks = buffer.at[0:count]
        pltpu.make_async_copy(blocks, blocks, sem).wait()

    def s_copy(it, off):
        return remote(
            s_all.at[it, gy], s_all.at[it, gy], ss.at[it], sr.at[it], along_y(off)
        )

    def z_copy(it, off):
        return remote(
            z_all.at[it, gx], z_all.at[it, gx], zs.at[it], zr.at[it], along_x(off)
        )

    def r_copy(off):
        to = along_z(off)
        return remote(r_send.at[to[2]], rblk.at[gz], rs, rr, to)

    def rp_copy(it, off):
        to = along_z(off)
        return remote(
            rp_send.at[it, to[2]], rp_all.at[it, gz], ps.at[it], pr.at[it], to
        )

    def m_copy(it):
        return remote(p_send.at[it], p_recv.at[it], ms.at[it], mr.at[it], mate)

    root_copy = remote(root_h, rinv2.at[1], xs, xr, mate)

    n = modes_n
    loads_c = None
    for it in range(ITERS):
        if it == 0:
            loaded["start"].wait()
            for j in range(8):
                local[j * block : (j + 1) * block, :] = start_v[perm[j]]
            loaded["op"].wait()
            right = local[...]
            for f in FACES:
                prod[it, f] = dot(op_v[inverse[f]], right)
            pl.semaphore_wait(barrier, len(greeted))
            on_faces(FACES, lambda f: halo_copy(it, f).start())
            on_faces(range(6), lambda f: modes_copy(f).start())
            root_copy.start()
            loaded["rinv"].wait()
            for b in range(nz):
                r_send[b] = jnp.concatenate(
                    [
                        rinv_v[:, a * width + b * n : a * width + (b + 1) * n]
                        for a in range(ny)
                    ],
                    axis=1,
                )
            for off in far_first(nz):
                r_copy(off).start()
            rblk[gz] = r_send[gz]
            for f in range(6):

                @pl.when(jnp.logical_not(has[f]))
                def _(f=f):
                    nbm[f] = jnp.zeros_like(nbm[f])
                    kb[f] = jnp.zeros_like(kb[f])
                    for it in range(ITERS):
                        halo[it, f] = jnp.zeros_like(halo[it, f])
            loaded["modes"].wait()
            loaded["loads"].wait()
            loaded["rw"].wait()
            modes_s[...] = split_rows(modes_v[...])
            modes_t[...] = deep_left(modes_v[...], modes_t.shape[1])
            g = jnp.dot(rw_v[...], modes_v[...], precision=HIGH, preferred_element_type=F32)
            g_t[...] = deep_left(g, g_t.shape[1])
            loaded["w"].wait()
            for f in range(8):
                wb[f] = jnp.broadcast_to(w_v[f : f + 1, :], (block, block)).T
            for k in range(nchip):
                for i in range(ITERS):
                    z_all[i, 2 * k + 1 - core] = jnp.zeros(z_all.shape[2:], F32)
            coarse = None
            for pair in (PAIRS[3], PAIRS[2], PAIRS[0], PAIRS[1]):
                for f in pair:
                    on_faces((f,), lambda f: halo_copy(it, f ^ 1).wait_recv())
                    whole = prod[it, f] + halo[it, f] if f < 6 else prod[it, f]
                    res[f] = loads_v[f].astype(F32) - whole
                f = pair[0]
                part = rows_dot(
                    modes_s[:, f * block : (f + 2) * block], res[f : f + 2].reshape(2 * block, -1)
                )
                coarse = part if coarse is None else coarse + part
        else:
            for j in range(8):
                local[j * block : (j + 1) * block, :] = solb[perm[j]]
            right = local[...]
            own = None
            for p, pair in enumerate(PAIRS):
                rows = op_f[pair[0] * block : (pair[0] + 2) * block, :]
                both = dot(rows, right)
                prod[it, pair[0]] = both[:block]
                prod[it, pair[1]] = both[block:]
                got = rows_dot_last(pair_s[p, : 3 * n * (3 if pair[0] < 6 else 1)], both)
                if pair[0] < 6:
                    kb_send[pair[0]] = got[n : 2 * n]
                    kb_send[pair[1]] = got[2 * n :]
                    on_faces(pair, lambda f: kb_copy(f).start())
                own = got[:n] if own is None else own + got[:n]
            on_faces((0, 1), lambda f: halo_copy(it, f).start())
            coarse = loads_c - own
            for f in (0, 1, 2, 3, 4, 5):
                on_faces((f,), lambda f: kb_copy(f ^ 1).wait_recv())
                coarse = coarse - kb[f]
        c_all[it, gy] = coarse
        t_all[it, gz] = jnp.dot(
            rw_v[...], coarse, precision=HIGH, preferred_element_type=F32
        )
        for off in far_first(nz):
            t_copy(it, off).start()
        for off in far_first(ny):
            c_copy(it, off).start()
        if it:
            on_faces((2, 3), lambda f: halo_copy(it, f).start())
        else:
            all_of(rblk, nz - 1, rr)
            rblk_s[...] = split_rows(rblk[...].reshape(rblk_s.shape[0] // 3, -1))
            root_copy.wait_recv()
            loaded["root"].wait()
            rinv_s[...] = split_rows(rinv2[...].reshape(rinv_s.shape[0] // 3, -1))
        all_of(c_all.at[it], ny - 1, cr.at[it])
        part = (rows_dot_last if it else rows_dot)(rblk_s[...], c_all[it].reshape(ny * n, -1))
        rp_send[it] = part.reshape(rp_send.shape[1:])
        all_of(t_all.at[it], nz - 1, tr.at[it])
        total = t_all[it, 0]
        for b in range(1, nz):
            total = total + t_all[it, b]
        s_all[it, gy] = total
        for off in far_first(ny):
            s_copy(it, off).start()
        for off in far_first(nz):
            rp_copy(it, off).start()
        rp_all[it, gz] = rp_send[it, gz]
        if it:
            on_faces((4, 5), lambda f: halo_copy(it, f).start())
        all_of(s_all.at[it], ny - 1, sr.at[it])
        total = s_all[it, 0]
        for a in range(1, ny):
            total = total + s_all[it, a]
        z_all[it, gx] = total
        for off in far_first(nchip):
            z_copy(it, off).start()
        for f in (6, 7, 0, 1, 2, 3, 4, 5):
            if it:
                on_faces((f,), lambda f: halo_copy(it, f ^ 1).wait_recv())
                whole = prod[it, f] + halo[it, f] if f < 6 else prod[it, f]
                rest = loads_v[f].astype(F32) - whole
                old = sol[f]
            else:
                rest = res[f]
                old = start_v[f].astype(F32)
            scale = wb[f]
            sol[f] = old + jnp.concatenate([scale] * (old.shape[1] // block), axis=1) * rest
        if it == 0:
            for f in range(8):
                op_f[f * block : (f + 1) * block, :] = op_v[inverse[f]]
            for f in range(8):
                got = dot(modes_s[:, f * block : (f + 1) * block], loads_v[f])
                loads_c = got if loads_c is None else loads_c + got
            loads_c = (loads_c[2 * n :] + loads_c[n : 2 * n]) + loads_c[:n]
            pair_s[3, : 3 * n] = modes_s[:, 6 * block :]
            fill = jnp.zeros((n, block), F32)
            for p in range(3):
                pair = PAIRS[p]
                on_faces(pair, lambda f: modes_copy(f ^ 1).wait_recv())
                pair_s[p] = split_rows(
                    jnp.concatenate([
                        modes_v[:, pair[0] * block : (pair[0] + 2) * block],
                        jnp.concatenate([nbm[pair[0]], fill], axis=1),
                        jnp.concatenate([fill, nbm[pair[1]]], axis=1),
                    ], axis=0)
                )
        all_of(rp_all.at[it], nz - 1, pr.at[it])
        region = rp_all[it, 0]
        for b in range(1, nz):
            region = region + rp_all[it, b]
        depth = modes_t.shape[1]
        with_region = sol[...] + dot(modes_t[...], deep_right(region, depth)).reshape(sol.shape)
        sol[...] = with_region
        if it == ITERS - 1:
            base_out = pltpu.make_async_copy(sol, base_o, out_sem.at[0])
            base_out.start()
            g_out = pltpu.make_async_copy(g_t, g_o, out_sem.at[1])
            g_out.start()
        if it == 0:
            on_faces(range(6), lambda f: modes_copy(f).wait_send())
            all_of(rblk, nz - 1, rs)
            root_copy.wait_send()
        else:
            on_faces(range(6), lambda f: kb_copy(f).wait_send())
            m_copy(it - 1).wait_send()
        on_faces(range(6), lambda f: halo_copy(it, f).wait_send())
        all_of(t_all.at[it], nz - 1, ts.at[it])
        all_of(rp_all.at[it], nz - 1, ps.at[it])
        all_of(s_all.at[it], ny - 1, ss.at[it])
        all_of(c_all.at[it], ny - 1, cs.at[it])
        all_of(z_all.at[it], nchip - 1, zr.at[it])
        stack = z_all[it].reshape(nx * z_all.shape[2], -1)
        both = (rows_dot_last if it else rows_dot)(rinv_s[...], stack)
        rm = both.shape[0] // 2
        p_send[it] = both[rm:]
        m_copy(it).start()
        all_of(z_all.at[it], nchip - 1, zs.at[it])
        m_copy(it).wait_recv()
        root = both[:rm] + p_recv[it]
        if it < ITERS - 1:
            depth = g_t.shape[1]
            new = sol[...] + dot(g_t[...], deep_right(root, depth)).reshape(sol.shape)
            sol[...] = new
            solb[...] = new.astype(BF16)
        else:
            root_v[...] = root
            root_out = pltpu.make_async_copy(root_v, root_o, out_sem.at[2])
            root_out.start()

    m_copy(ITERS - 1).wait_send()
    base_out.wait()
    g_out.wait()
    root_out.wait()


def last_update(base, g, root, out_h, out, sem):
    right = deep_right(root[...], g.shape[1])
    steps, rows = out.shape[0], out.shape[1]
    sent = []
    for i in range(steps):
        at = slice(i * rows, (i + 1) * rows)
        out[i] = base[at] + dot(g[at], right)
        sent.append(pltpu.make_async_copy(out.at[i], out_h.at[i], sem.at[i]))
        sent[-1].start()
    for copy in sent:
        copy.wait()


def per_device(
    nx, ny, nz, loads, start, interface_op, block_order, interface_weights, coarse_modes,
    region_weights, region_inverse, root_inverse,
):
    iface, cases = loads.shape[-2:]
    block = iface // 8
    modes_n, rm = region_weights.shape[-2:]
    nchip = nx // 2
    width = nz * modes_n
    faces = (8, block, cases)
    deep_m, deep_g = pad_to(6 * modes_n, 128), pad_to(6 * rm, 128)
    hbm_spec = pl.BlockSpec(memory_space=pltpu.HBM)
    vmem_spec = pl.BlockSpec(memory_space=pltpu.VMEM)
    dma = pltpu.SemaphoreType.DMA
    base, g, root = pl.pallas_call(
        functools.partial(kernel, nx, ny, nz),
        out_shape=(
            jax.ShapeDtypeStruct(faces, F32),
            jax.ShapeDtypeStruct((iface, deep_g), BF16),
            jax.ShapeDtypeStruct((rm, cases), F32),
        ),
        in_specs=[hbm_spec] * 9,
        out_specs=(hbm_spec,) * 3,
        scratch_shapes=[
            pltpu.SMEM((8,), jnp.int32),
            pltpu.VMEM(faces, BF16),
            pltpu.VMEM(faces, BF16),
            pltpu.VMEM((8, block, iface), BF16),
            pltpu.VMEM((iface, iface), BF16),
            pltpu.VMEM((8, block), F32),
            pltpu.VMEM((modes_n, iface), F32),
            pltpu.VMEM((rm, modes_n), F32),
            pltpu.VMEM((modes_n, ny * width), F32),
            pltpu.VMEM((nz, modes_n, ny * modes_n), F32),
            pltpu.VMEM((iface, cases), BF16),
            pltpu.VMEM((ITERS, *faces), F32),
            pltpu.VMEM((ITERS, 6, block, cases), F32),
            pltpu.VMEM(faces, F32),
            pltpu.VMEM(faces, BF16),
            pltpu.VMEM(faces, F32),
            pltpu.VMEM((8, block, block), F32),
            pltpu.VMEM((3 * modes_n, iface), BF16),
            pltpu.VMEM((4, 9 * modes_n, 2 * block), BF16),
            pltpu.VMEM((iface, deep_m), BF16),
            pltpu.VMEM((iface, deep_g), BF16),
            pltpu.VMEM((6, modes_n, block), F32),
            pltpu.VMEM((nz, modes_n, ny * modes_n), F32),
            pltpu.VMEM((3 * width, ny * modes_n), BF16),
            pltpu.VMEM((2, rm, nx * rm), F32),
            pltpu.VMEM((6 * rm, nx * rm), BF16),
            pltpu.VMEM((6, modes_n, cases), F32),
            pltpu.VMEM((6, modes_n, cases), F32),
            pltpu.VMEM((ITERS, nz, rm, cases), F32),
            pltpu.VMEM((ITERS, ny, modes_n, cases), F32),
            pltpu.VMEM((ITERS, ny, rm, cases), F32),
            pltpu.VMEM((ITERS, nz, modes_n, cases), F32),
            pltpu.VMEM((ITERS, nz, modes_n, cases), F32),
            pltpu.VMEM((ITERS, nx, rm, cases), F32),
            pltpu.VMEM((ITERS, rm, cases), F32),
            pltpu.VMEM((ITERS, rm, cases), F32),
            dma((9,)),
            dma((ITERS, 6)), dma((ITERS, 6)),
            dma((6,)), dma((6,)),
            dma((6,)), dma((6,)),
            dma((ITERS,)), dma((ITERS,)),
            dma((ITERS,)), dma((ITERS,)),
            dma((ITERS,)), dma((ITERS,)),
            dma((ITERS,)), dma((ITERS,)),
            dma(()), dma(()),
            dma((ITERS,)), dma((ITERS,)),
            dma((ITERS,)), dma((ITERS,)),
            dma(()), dma(()),
            pltpu.VMEM((rm, cases), F32),
            dma((3,)),
        ],
        compiler_params=pltpu.CompilerParams(
            collective_id=0, has_side_effects=True, vmem_limit_bytes=44 * 2**20
        ),
        name="iterate",
    )(
        *(
            pltpu.with_memory_space_constraint(x, pltpu.HBM)
            for x in (
                block_order.reshape(8),
                loads.reshape(faces),
                start.reshape(faces),
                interface_op.reshape(8, block, iface),
                interface_weights.reshape(8, block),
                coarse_modes.reshape(modes_n, iface),
                region_weights.reshape(modes_n, rm).T,
                region_inverse.reshape(modes_n, -1),
                root_inverse,
            )
        )
    )
    rows = (4, iface // 4, cases)
    out = pl.pallas_call(
        last_update,
        out_shape=jax.ShapeDtypeStruct(rows, F32),
        in_specs=[vmem_spec] * 3,
        out_specs=hbm_spec,
        scratch_shapes=[pltpu.VMEM(rows, F32), dma((4,))],
        compiler_params=pltpu.CompilerParams(vmem_limit_bytes=16 * 2**20),
        name="last_update",
    )(base.reshape(iface, cases), g, root)
    return out.reshape(1, 1, 1, iface, cases)


def solution(mesh):
    nx, ny, nz = (mesh.shape[axis] for axis in ("gx", "gy", "gz"))
    placed = (
        P("gx", "gy", "gz", None, None),
        P("gx", "gy", "gz", None, None),
        P("gx", "gy", "gz", None, None),
        P("gx", "gy", "gz", None),
        P("gx", "gy", "gz", None),
        P("gx", "gy", "gz", None, None),
        P("gx", "gy", "gz", None, None),
        P("gx", ("gy", "gz"), None),
        P("gx", None),
    )
    return jax.shard_map(
        functools.partial(per_device, nx, ny, nz),
        mesh=mesh,
        in_specs=placed,
        out_specs=P("gx", "gy", "gz", None, None),
        check_vma=False,
    )
```
